256 devices in a mesh: dp: 16 (over x, y), seq: 16 (over z, core).
Axes of the slice: x: 4, y: 4, z: 8, core: 2. Of those that a mesh axis runs over, the one named last changes fastest.
Arguments:
- tokens: bfloat16 [16, 16, 32, 4, 512], P('dp', 'seq'), may hold values from -6 to 6
- conv_first: bfloat16 [27, 512, 128], replicated, may hold values from -0.0546875 to 0.0546875
- bias_first: float32 [128], replicated, may hold values from -3 to 3
- conv_second: bfloat16 [27, 128, 384], replicated, may hold values from -0.109375 to 0.109375
- bias_second: float32 [384], replicated, may hold values from -3 to 3
- pixels: bfloat16 [16, 16, 32, 4, 1536], P('dp', None, 'seq'), may hold values from 0 to 1
- mask_index: int32 [16, 115], P('dp'), may hold values from 0 to 127, as said below
Outputs:
- grad_first: float32 [27, 512, 128], P(None, 'seq', 'dp')
- grad_second: float32 [27, 128, 384], P(None, 'seq', 'dp')
The draws below stay inside these ranges and needn't reach their ends.
Inputs may be any that keep to these rules, and one draw needn't show every extreme that they name: `mask_index`: each row holds 115 distinct positions of the 32 x 4 token grid.
All inputs are finite; a program needn't handle non-finite values.
Results may differ from the reference program's by a relative error of at most 0.003.
Values may be sent and summed in bfloat16 or wider, within the bound.
No kernel may reach another device: no remote copies, remote signals or barrier semaphores. Data moves between devices by JAX's collectives and lax.ppermute only.
A program may use at most 128 MiB of HBM per device.

```python
from functools import partial
import jax
import jax.numpy as jnp
from jax import lax

D = 512
C1 = 128
CO = 384
T_SIZE = 16
W = 4
H = 32
CLIPS = 16
MASKED = 115


def draw_mask_index(key, part):
    clip_keys = jax.random.split(jax.random.fold_in(key, 17), CLIPS)
    orders = jax.vmap(lambda one_key: jax.random.permutation(one_key, H * W))(clip_keys)
    return orders[:, :MASKED].astype(jnp.int32)


def level_of(own_key, shape, cuts, low, high):
    loudness, own = 1.0, jax.random.fold_in(own_key, 6)
    for position, blocks in cuts:
        heights = jnp.exp(jax.random.uniform(jax.random.fold_in(own, position), (blocks,), jnp.float32, low / len(cuts), high / len(cuts)))
        loudness = loudness * jnp.repeat(heights, shape[position] // blocks).reshape([-1 if axis == position else 1 for axis in range(len(shape))])
    return loudness


def gaussian(own_key, extent, scale, limit, cuts=(), kind=jnp.bfloat16):
    level = level_of(own_key, extent, cuts, -0.22, 0.18) if cuts else 1.0
    drawn = jax.random.normal(own_key, extent, jnp.float32) * scale * level
    return jnp.minimum(jnp.maximum(drawn, -limit), limit).astype(kind)


def setup_inputs(seed: int = 0) -> dict:
    key_list = jax.random.split(jax.random.key(seed), 8)
    return {
        "tokens": gaussian(key_list[0], (CLIPS, T_SIZE, H, W, D), 1.0, 6.0, ((0, 16), (1, 16))),
        "conv_first": gaussian(key_list[1], (27, D, C1), (27 * D) ** -0.5, 0.0546875),
        "bias_first": gaussian(key_list[2], (C1,), 0.5, 3.0, (), jnp.float32),
        "conv_second": gaussian(key_list[3], (27, C1, CO), (27 * C1) ** -0.5, 0.109375),
        "bias_second": gaussian(key_list[4], (CO,), 0.5, 3.0, (), jnp.float32),
        "pixels": jnp.clip(1.0 * jax.random.uniform(key_list[5], (CLIPS, T_SIZE, H, W, 4 * CO), jnp.float32) ** level_of(key_list[5], (CLIPS, T_SIZE, H, W, 4 * CO), ((0, 16), (2, 16)), -0.2, 0.2), 0.0, 1.0).astype(jnp.bfloat16),
        "mask_index": draw_mask_index(jax.random.fold_in(key_list[7], 71), 0),
    }


def shifts_of(tap_index):
    return (tap_index // 9, tap_index // 3 % 3, tap_index % 3)

def pad_full(field):
    return jnp.pad(field, ((1, 1), (1, 1), (1, 1), (0, 0)))

def conv_taps(padded, weight):
    frames = padded.shape[0] - 2
    rows = padded.shape[1] - 2
    cols = padded.shape[2] - 2
    summed = jnp.zeros((frames * rows * cols, weight.shape[2]), jnp.float32)
    for tap_index in range(27):
        shift_time, shift_row, shift_col = shifts_of(tap_index)
        window = padded[shift_time:shift_time + frames, shift_row:shift_row + rows, shift_col:shift_col + cols]
        summed = summed + jnp.dot(window.reshape(-1, padded.shape[3]), weight[tap_index], preferred_element_type=jnp.float32)
    return summed.reshape(frames, rows, cols, weight.shape[2])

def tap_grads(padded, cotangent):
    frames, rows, cols, width = cotangent.shape
    flat = cotangent.reshape(-1, width)
    result = []
    for tap_index in range(27):
        shift_time, shift_row, shift_col = shifts_of(tap_index)
        window = padded[shift_time:shift_time + frames, shift_row:shift_row + rows, shift_col:shift_col + cols]
        result.append(lax.dot_general(window.reshape(-1, padded.shape[3]), flat, (((0,), (0,)), ((), ())), preferred_element_type=jnp.float32))
    return jnp.stack(result)

def conv_back(padded, weight):
    frames = padded.shape[0] - 2
    rows = padded.shape[1] - 2
    cols = padded.shape[2] - 2
    summed = jnp.zeros((frames * rows * cols, weight.shape[1]), jnp.float32)
    for tap_index in range(27):
        shift_time, shift_row, shift_col = shifts_of(tap_index)
        window = padded[2 - shift_time:2 - shift_time + frames, 2 - shift_row:2 - shift_row + rows, 2 - shift_col:2 - shift_col + cols]
        summed = summed + lax.dot_general(window.reshape(-1, padded.shape[3]), weight[tap_index], (((1,), (1,)), ((), ())), preferred_element_type=jnp.float32)
    return summed.reshape(frames, rows, cols, weight.shape[1])

def reference(tokens, conv_first, bias_first, conv_second, bias_second, pixels, mask_index):
    gelu_tanh = partial(jax.nn.gelu, approximate=True)

    def per_clip(carry, inputs):
        clip_tokens, clip_pixels, clip_index = inputs
        frames, rows, cols, width = clip_tokens.shape
        tokens_padded = pad_full(clip_tokens)
        zsum = conv_taps(tokens_padded, conv_first) + bias_first
        hidden = gelu_tanh(zsum).astype(jnp.bfloat16)
        upsampled = jnp.repeat(jnp.repeat(hidden, 2, axis=1), 2, axis=2)
        up_padded = pad_full(upsampled)
        predict = conv_taps(up_padded, conv_second) + bias_second
        values = predict.shape[3]
        pix = clip_pixels.astype(jnp.float32)
        center = pix - lax.optimization_barrier(jnp.mean(pix, axis=-1, keepdims=True))
        spread = lax.optimization_barrier(jnp.mean(center * center, axis=-1, keepdims=True))
        normed = center * lax.rsqrt(spread + 1e-06)
        normed = normed.reshape(frames, rows, cols, 2, 2, values).transpose(0, 1, 3, 2, 4, 5).reshape(frames, 2 * rows, 2 * cols, values)
        positions = jnp.arange(rows * cols, dtype=jnp.int32)
        hits = lax.optimization_barrier(jnp.sum((positions[:, None] == clip_index[None, :]).astype(jnp.float32), axis=1)).reshape(rows, cols)
        cell_mask = jnp.repeat(jnp.repeat(hits, 2, axis=0), 2, axis=1)
        cotangent = (2.0 / (4 * values) * cell_mask[None, :, :, None] * (predict - normed)).astype(jnp.bfloat16)
        grad_second = tap_grads(up_padded, cotangent)
        grad_up = conv_back(pad_full(cotangent), conv_second)
        grad_hidden = grad_up.reshape(frames, rows, 2, cols, 2, grad_up.shape[3]).sum(axis=(2, 4))
        grad_z = jax.vjp(gelu_tanh, zsum)[1](grad_hidden)[0].astype(jnp.bfloat16)
        grad_first = tap_grads(tokens_padded, grad_z)
        return ((carry[0] + grad_first, carry[1] + grad_second), None)
    start = (jnp.zeros(conv_first.shape, jnp.float32), jnp.zeros(conv_second.shape, jnp.float32))
    final, unused = lax.scan(per_clip, start, (tokens, pixels, mask_index))
    return (final[0], final[1])
```

```python
from functools import partial

import jax
import jax.numpy as jnp
from jax import lax
from jax.experimental import pallas as pl
from jax.experimental.pallas import tpu as pltpu
from jax.sharding import PartitionSpec as P

F32 = jnp.float32
BF16 = jnp.bfloat16
POS, COLS, PAD = 128, 4, 8
D, C1, CO = 512, 128, 384
TAPS9 = [(row, col) for row in range(3) for col in range(3)]
PHASES = [(i, j) for i in range(2) for j in range(2)]
PAIRS = [(-1, 1), (0, 0), (0, 1), (1, 0)]
PAIRS_OF_TAP = [[(0, 1), (1, 0)], [(0, 0), (0, 1)], [(-1, 1), (0, 0)]]


def token_step(phase, tap):
    return (phase + tap - 1) // 2


def column_mask(step, shape, axis):
    column = lax.broadcasted_iota(jnp.int32, shape, axis) % COLS + step
    return (column >= 0) & (column < COLS)


def spot_mask(row_step, col_step, shape, axis):
    spot = lax.broadcasted_iota(jnp.int32, shape, axis)
    column = spot % COLS + col_step
    row = spot // COLS + row_step
    return (column >= 0) & (column < COLS) & (row >= 0) & (row < POS // COLS)


def call(body, out_shape, scratch=(), flops=0, size=0):
    return pl.pallas_call(
        body,
        out_shape=out_shape,
        scratch_shapes=list(scratch),
        compiler_params=pltpu.CompilerParams(vmem_limit_bytes=48 << 20),
        cost_estimate=pl.CostEstimate(flops=flops, bytes_accessed=size, transcendentals=0),
    )


def struct(shape, dtype):
    return jax.ShapeDtypeStruct(shape, dtype)


def first_conv(tokens_ref, weight_ref, y0_ref, y1_ref, y2_ref, turned_ref, padded):
    padded[0:PAD] = jnp.zeros((PAD, D), F32)
    padded[PAD + POS :] = jnp.zeros((PAD, D), F32)
    tokens = tokens_ref[...]
    padded[PAD : PAD + POS] = tokens.astype(F32)
    total = jnp.zeros((POS, 3 * C1), F32)
    for row, col in TAPS9:
        step = PAD + COLS * (row - 1) + col - 1
        window = padded[step : step + POS]
        if col != 1:
            window = jnp.where(column_mask(col - 1, (POS, D), 0), window, 0.0)
        tap = 3 * row + col
        weight = jnp.concatenate([weight_ref[tap + 9 * k] for k in range(3)], axis=1)
        total = total + jnp.dot(window.astype(BF16), weight, preferred_element_type=F32)
    y0_ref[...] = total[:, 0:C1]
    y1_ref[...] = total[:, C1 : 2 * C1]
    y2_ref[...] = total[:, 2 * C1 :]
    turned_ref[...] = tokens.T


def tap_weight(weight_ref, row, col):
    return jnp.concatenate([weight_ref[9 * k + 3 * row + col] for k in range(3)], axis=0)


def loss_cotangent(before_ref, here_ref, after_ref, weight_ref, bias_ref, pixel_ref, index_ref,
                   cot_ref, turned_ref, padded, moved):
    zeros = jnp.zeros((PAD, 3 * C1), F32)
    padded[0:PAD] = zeros
    padded[PAD + POS :] = zeros
    for k, ref in enumerate((before_ref, here_ref, after_ref)):
        padded[PAD : PAD + POS, k * C1 : (k + 1) * C1] = ref[...].astype(F32)
    for row, col in TAPS9:
        step = PAD + COLS * (row - 1) + col - 1
        window = padded[step : step + POS]
        if col != 1:
            window = jnp.where(column_mask(col - 1, (POS, 3 * C1), 0), window, 0.0)
        moved[3 * row + col] = window.astype(BF16)
    predict = jnp.zeros((4 * POS, CO), F32)
    for row, col in TAPS9:
        lhs = jnp.concatenate(
            [moved[3 * (token_step(i, row) + 1) + token_step(j, col) + 1] for i, j in PHASES], axis=0
        )
        predict = predict + jnp.dot(
            lhs, tap_weight(weight_ref, row, col), preferred_element_type=F32
        )
    predict = predict + bias_ref[...]
    pix = pixel_ref[...].astype(F32)
    center = pix - jnp.mean(pix, axis=-1, keepdims=True)
    spread = jnp.mean(center * center, axis=-1, keepdims=True)
    normed = center * lax.rsqrt(spread + 1e-06)
    spot = lax.broadcasted_iota(jnp.int32, (POS, index_ref.shape[1]), 0)
    hits = jnp.sum((spot == index_ref[...]).astype(F32), axis=1, keepdims=True)
    scale = (2.0 / (4 * CO)) * hits
    turned = []
    for k in range(4):
        cot = scale * (predict[k * POS : (k + 1) * POS] - normed[:, k * CO : (k + 1) * CO])
        cot = cot.astype(BF16)
        cot_ref[k * POS : (k + 1) * POS] = cot
        turned.append(cot.astype(F32).T)
    width = CO // 16
    for block in range(16):
        turned_ref[block] = jnp.concatenate(
            [part[block * width : (block + 1) * width] for part in turned], axis=0
        ).astype(BF16)


def back_conv(cot_ref, weight_ref, u0_ref, u1_ref, u2_ref, padded):
    cot = cot_ref[...]
    sums = {}
    for row, col in TAPS9:
        part = lax.dot_general(
            cot, tap_weight(weight_ref, row, col), (((1,), (1,)), ((), ())),
            preferred_element_type=F32,
        )
        for k, (i, j) in enumerate(PHASES):
            key = (token_step(i, row), token_step(j, col))
            piece = part[k * POS : (k + 1) * POS]
            sums[key] = sums[key] + piece if key in sums else piece
    zeros = jnp.zeros((PAD, 3 * C1), F32)
    total = sums[(0, 0)]
    for k, ((row, col), value) in enumerate(sums.items()):
        if (row, col) == (0, 0):
            continue
        if col != 0:
            value = jnp.where(column_mask(col, (POS, 3 * C1), 0), value, 0.0)
        padded[k, 0:PAD] = zeros
        padded[k, PAD + POS :] = zeros
        padded[k, PAD : PAD + POS] = value
        step = PAD - COLS * row - col
        total = total + padded[k, step : step + POS]
    u0_ref[...] = total[:, 0:C1]
    u1_ref[...] = total[:, C1 : 2 * C1]
    u2_ref[...] = total[:, 2 * C1 :]


def second_grads(before_ref, here_ref, after_ref, turned_ref, out_ref, left):
    clips = turned_ref.shape[0]
    width = CO // 16
    masks = {}
    for row in (-1, 0, 1):
        for col in (-1, 0, 1):
            masks[(row, col)] = spot_mask(row, col, (width, POS), 1)
    for clip in range(clips):
        values = turned_ref[clip].astype(F32)
        parts = []
        for row, i in PAIRS:
            for col, j in PAIRS:
                k = 2 * i + j
                value = values[k * width : (k + 1) * width]
                step = COLS * row + col
                if step != 0:
                    value = pltpu.roll(value, (POS - step) % POS, 1)
                    value = jnp.where(masks[(row, col)], value, 0.0)
                parts.append(value)
        left[:, clip * POS : (clip + 1) * POS] = jnp.concatenate(parts, axis=0).astype(BF16)
    right = jnp.concatenate(
        [ref[...].reshape(clips * POS, C1) for ref in (before_ref, here_ref, after_ref)], axis=1
    )
    both = jnp.dot(left[...], right, preferred_element_type=F32)
    parts = []
    for k in range(3):
        for row in range(3):
            for col in range(3):
                value = None
                for row_pair in PAIRS_OF_TAP[row]:
                    for col_pair in PAIRS_OF_TAP[col]:
                        at = 4 * PAIRS.index(row_pair) + PAIRS.index(col_pair)
                        piece = both[at * width : (at + 1) * width, k * C1 : (k + 1) * C1]
                        value = piece if value is None else value + piece
                parts.append(value)
    parts.append(jnp.zeros((6 * 128 - 27 * width, C1), F32))
    turned = jnp.concatenate(parts, axis=0).T
    out_ref[...] = turned.reshape(out_ref.shape)


def moved_tokens(tokens_ref, out_ref):
    frames, width, _ = tokens_ref.shape
    zeros = jnp.zeros((9 * width, POS), BF16)
    out_ref[:, 0:POS] = zeros
    out_ref[:, (frames + 1) * POS :] = zeros
    for frame in range(frames):
        value = tokens_ref[frame].astype(F32)
        parts = []
        for row, col in TAPS9:
            step = COLS * (row - 1) + col - 1
            if step == 0:
                parts.append(value)
            else:
                part = pltpu.roll(value, (POS - step) % POS, 1)
                parts.append(
                    jnp.where(spot_mask(row - 1, col - 1, (width, POS), 1), part, 0.0)
                )
        out_ref[:, (frame + 1) * POS : (frame + 2) * POS] = jnp.concatenate(parts, axis=0).astype(
            BF16
        )


def first_grads(moved_ref, gz_ref, out_ref):
    frames = gz_ref.shape[0]
    right = gz_ref[...].reshape(frames * POS, C1)
    parts = []
    for k in range(3):
        parts.append(
            jnp.dot(
                moved_ref[:, k * POS : (k + frames) * POS], right, preferred_element_type=F32
            )
        )
    rows = 3 * parts[0].shape[0]
    parts.append(jnp.zeros((out_ref.shape[2] - rows, C1), F32))
    turned = jnp.concatenate(parts, axis=0).T
    out_ref[...] = turned.reshape(out_ref.shape)


def summed_second(parts_ref, out_ref):
    total = jnp.sum(parts_ref[...], axis=0)
    width = out_ref.shape[2]
    for k in range(27):
        out_ref[k] = total[:, k * width : (k + 1) * width]


def summed_first(parts_ref, out_ref):
    total = jnp.sum(parts_ref[...], axis=0)
    high, wide = total.shape
    total = jnp.concatenate([total, jnp.zeros((128 - high, wide), F32)], axis=0)
    turned = total.T
    width = out_ref.shape[1]
    for k in range(27):
        out_ref[k] = turned[k * width : (k + 1) * width, 0:high]


def exchange(value, axis):
    return lax.all_to_all(value, axis, split_axis=0, concat_axis=0, tiled=True)


def up(value, axis="seq"):
    count = lax.axis_size(axis)
    return lax.ppermute(value, axis, [(i, i + 1) for i in range(count - 1)])


def down(value, axis="seq"):
    count = lax.axis_size(axis)
    return lax.ppermute(value, axis, [(i + 1, i) for i in range(count - 1)])


def per_device(tokens, conv_first, bias_first, conv_second, bias_second, pixels, mask_index):
    gelu_tanh = partial(jax.nn.gelu, approximate=True)
    field = tokens.reshape(POS, D)
    pix = exchange(pixels[0], "seq").reshape(POS, 4 * CO)

    plane = struct((POS, C1), F32)
    y0, y1, y2, turned = call(
        first_conv,
        (plane, plane, plane, struct((D, POS), BF16)),
        [pltpu.VMEM((POS + 2 * PAD, D), F32)],
        flops=2 * POS * 27 * D * C1,
        size=4 << 20,
    )(field, conv_first)
    zsum = up(y0) + y1 + down(y2) + bias_first
    hidden = gelu_tanh(zsum).astype(BF16)
    before, after = up(hidden), down(hidden)
    hidden_all = exchange(jnp.broadcast_to(hidden[None], (16, POS, C1)), "dp")

    cot, cot_turned = call(
        loss_cotangent,
        (struct((4 * POS, CO), BF16), struct((16, CO // 4, POS), BF16)),
        [pltpu.VMEM((POS + 2 * PAD, 3 * C1), F32), pltpu.VMEM((9, POS, 3 * C1), BF16)],
        flops=2 * 4 * POS * 27 * C1 * CO,
        size=4 << 20,
    )(before, hidden, after, conv_second, bias_second[None], pix, mask_index)
    u0, u1, u2 = call(
        back_conv,
        (plane, plane, plane),
        [pltpu.VMEM((9, POS + 2 * PAD, 3 * C1), F32)],
        flops=2 * 4 * POS * 27 * C1 * CO,
        size=4 << 20,
    )(cot, conv_second)
    grad_hidden = down(u0) + u1 + up(u2)
    grad_z = jax.vjp(gelu_tanh, zsum)[1](grad_hidden)[0].astype(BF16)

    cot_all = exchange(cot_turned, "dp")
    grad_z_all = exchange(jnp.broadcast_to(grad_z[None], (16, POS, C1)), "seq")
    part_second = call(
        second_grads,
        struct((16, C1 // 16, 6 * 128), F32),
        [pltpu.VMEM((CO, 16 * POS), BF16)],
        flops=2 * 16 * POS * CO * CO,
        size=3 << 20,
    )(up(hidden_all), hidden_all, down(hidden_all), cot_all)
    all_second = exchange(part_second, "seq")

    token_part = exchange(turned.reshape(16, D // 16, POS), "seq")
    moved = call(
        moved_tokens, struct((9 * D // 16, 18 * POS), BF16), flops=1 << 20, size=2 << 20
    )(token_part)
    part_first = call(
        first_grads,
        struct((16, C1 // 16, 7 * 128), F32),
        flops=2 * 16 * POS * 27 * C1 * D // 16,
        size=3 << 20,
    )(moved, grad_z_all)
    all_first = exchange(part_first, "dp")

    grad_first = call(summed_first, struct((27, D // 16, C1 // 16), F32), size=1 << 20)(all_first)
    grad_second = call(summed_second, struct((27, C1 // 16, CO // 16), F32), size=1 << 20)(
        all_second
    )
    return grad_first, grad_second


def solution(mesh):
    return jax.shard_map(
        per_device,
        mesh=mesh,
        in_specs=(
            P("dp", "seq", None, None, None),
            P(),
            P(),
            P(),
            P(),
            P("dp", None, "seq", None, None),
            P("dp", None),
        ),
        out_specs=(P(None, "seq", "dp"), P(None, "seq", "dp")),
        check_vma=False,
    )
```

```python
from functools import partial

import jax
import jax.numpy as jnp
from jax import lax
from jax.experimental import pallas as pl
from jax.experimental.pallas import tpu as pltpu
from jax.sharding import PartitionSpec as P

F32 = jnp.float32
BF16 = jnp.bfloat16
POS, COLS, PAD = 128, 4, 8
D, C1, CO = 512, 128, 384
CHUNK = 4 * CO // 16
TAPS9 = [(row, col) for row in range(3) for col in range(3)]
PHASES = [(i, j) for i in range(2) for j in range(2)]
PAIRS = [(-1, 1), (0, 0), (0, 1), (1, 0)]
PAIRS_OF_TAP = [[(0, 1), (1, 0)], [(0, 0), (0, 1)], [(-1, 1), (0, 0)]]


def token_step(phase, tap):
    return (phase + tap - 1) // 2


def column_mask(step, shape, axis):
    column = lax.broadcasted_iota(jnp.int32, shape, axis) % COLS + step
    return (column >= 0) & (column < COLS)


def spot_mask(row_step, col_step, shape, axis):
    spot = lax.broadcasted_iota(jnp.int32, shape, axis)
    column = spot % COLS + col_step
    row = spot // COLS + row_step
    return (column >= 0) & (column < COLS) & (row >= 0) & (row < POS // COLS)


def call(body, out_shape, in_specs, scratch=(), flops=0, size=0, limit=16):
    return pl.pallas_call(
        body,
        out_shape=out_shape,
        in_specs=in_specs,
        scratch_shapes=list(scratch),
        compiler_params=pltpu.CompilerParams(vmem_limit_bytes=limit << 20),
        cost_estimate=pl.CostEstimate(flops=flops, bytes_accessed=size, transcendentals=0),
    )


def struct(shape, dtype):
    return jax.ShapeDtypeStruct(shape, dtype)


SMEM, VMEM, HBM = pltpu.SMEM, pltpu.VMEM, pltpu.HBM


def spots(*kinds):
    return [pl.BlockSpec(memory_space=kind) for kind in kinds]


def packed_inputs(pixel_ref, tokens_ref, out_ref):
    turned = tokens_ref[...].T
    width = D // 16
    for block in range(16):
        pix = pixel_ref[block].astype(F32)
        out_ref[block, 0:CHUNK] = jnp.concatenate(
            [pix[:, n * 128 : (n + 1) * 128] for n in range(4 * CO // 128)], axis=0
        ).astype(BF16)
        out_ref[block, CHUNK:] = turned[block * width : (block + 1) * width]


def first_conv(place_ref, tokens_ref, weight_ref, pair_ref, keep_ref, cross_ref, padded):
    padded[0:PAD] = jnp.zeros((PAD, D), F32)
    padded[PAD + POS :] = jnp.zeros((PAD, D), F32)
    padded[PAD : PAD + POS] = tokens_ref[...].astype(F32)
    total = jnp.zeros((POS, 3 * C1), F32)
    for row, col in TAPS9:
        step = PAD + COLS * (row - 1) + col - 1
        window = padded[step : step + POS]
        if col != 1:
            window = jnp.where(column_mask(col - 1, (POS, D), 0), window, 0.0)
        tap = 3 * row + col
        weight = jnp.concatenate([weight_ref[tap + 9 * k] for k in range(3)], axis=1)
        total = total + jnp.dot(window.astype(BF16), weight, preferred_element_type=F32)
    to_next, to_last = total[:, 0:C1], total[:, 2 * C1 :]
    even = place_ref[0] == 0
    pair_ref[...] = jnp.where(even, to_next, to_last)
    keep_ref[...] = total[:, C1 : 2 * C1]
    cross_ref[...] = jnp.where(even, to_last, to_next)


def tap_weight(weight_ref, row, col):
    return jnp.concatenate([weight_ref[9 * k + 3 * row + col] for k in range(3)], axis=0)


def loss_and_back(place_ref, pair_ref, here_ref, cross_ref, weight_ref, bias_ref, packed_ref,
                  index_ref, blocks_ref, to_pair_ref, keep_ref, to_cross_ref,
                  padded, moved, cots, shifted):
    even = place_ref[0] == 0
    zeros = jnp.zeros((PAD, 3 * C1), F32)
    padded[0:PAD] = zeros
    padded[PAD + POS :] = zeros
    pair, cross = pair_ref[...].astype(F32), cross_ref[...].astype(F32)
    frames = (jnp.where(even, cross, pair), here_ref[...].astype(F32), jnp.where(even, pair, cross))
    for k, value in enumerate(frames):
        padded[PAD : PAD + POS, k * C1 : (k + 1) * C1] = value
        narrow = value.astype(BF16)
        for block in range(16):
            blocks_ref[block, CHUNK + k * POS : CHUNK + (k + 1) * POS] = narrow
    for row, col in TAPS9:
        step = PAD + COLS * (row - 1) + col - 1
        window = padded[step : step + POS]
        if col != 1:
            window = jnp.where(column_mask(col - 1, (POS, 3 * C1), 0), window, 0.0)
        moved[3 * row + col] = window.astype(BF16)
    slabs = []
    for slab in range(16):
        part = packed_ref[slab, 0:CHUNK].astype(F32)
        slabs.append(
            jnp.concatenate([part[8 * n : 8 * n + 8] for n in range(4 * CO // 128)], axis=1)
        )
    pix = jnp.concatenate(slabs, axis=0)
    center = pix - jnp.mean(pix, axis=-1, keepdims=True)
    spread = jnp.mean(center * center, axis=-1, keepdims=True)
    normed = center * lax.rsqrt(spread + 1e-06)
    spot = lax.broadcasted_iota(jnp.int32, (POS, index_ref.shape[1]), 0)
    hits = jnp.sum((spot == index_ref[...]).astype(F32), axis=1, keepdims=True)
    scale = (2.0 / (4 * CO)) * hits
    predict = jnp.zeros((4 * POS, CO), F32)
    for row, col in TAPS9:
        lhs = jnp.concatenate(
            [moved[3 * (token_step(i, row) + 1) + token_step(j, col) + 1] for i, j in PHASES], axis=0
        )
        predict = predict + jnp.dot(
            lhs, tap_weight(weight_ref, row, col), preferred_element_type=F32
        )
    predict = predict + bias_ref[...]
    turned = []
    for k in range(4):
        cot = scale * (predict[k * POS : (k + 1) * POS] - normed[:, k * CO : (k + 1) * CO])
        cot = cot.astype(BF16)
        cots[k * POS : (k + 1) * POS] = cot
        turned.append(cot.astype(F32).T)
    width = CO // 16
    for block in range(16):
        blocks_ref[block, 0:CHUNK] = jnp.concatenate(
            [part[block * width : (block + 1) * width] for part in turned], axis=0
        ).astype(BF16)

    cot = cots[...]
    sums = {}
    for row, col in TAPS9:
        part = lax.dot_general(
            cot, tap_weight(weight_ref, row, col), (((1,), (1,)), ((), ())),
            preferred_element_type=F32,
        )
        for k, (i, j) in enumerate(PHASES):
            key = (token_step(i, row), token_step(j, col))
            piece = part[k * POS : (k + 1) * POS]
            sums[key] = sums[key] + piece if key in sums else piece
    total = sums[(0, 0)]
    for k, ((row, col), value) in enumerate(sums.items()):
        if (row, col) == (0, 0):
            continue
        if col != 0:
            value = jnp.where(column_mask(col, (POS, 3 * C1), 0), value, 0.0)
        shifted[k, 0:PAD] = zeros
        shifted[k, PAD + POS :] = zeros
        shifted[k, PAD : PAD + POS] = value
        step = PAD - COLS * row - col
        total = total + shifted[k, step : step + POS]
    to_last, to_next = total[:, 0:C1], total[:, 2 * C1 :]
    to_pair_ref[...] = jnp.where(even, to_next, to_last)
    keep_ref[...] = total[:, C1 : 2 * C1]
    to_cross_ref[...] = jnp.where(even, to_last, to_next)


def second_grads(blocks_ref, out_ref, left, right):
    wide, thin = CO // 16, C1 // 16
    masks = {}
    for row in (-1, 0, 1):
        for col in (-1, 0, 1):
            masks[(row, col)] = spot_mask(row, col, (1, POS), 1)
    for clip in range(16):
        lanes = slice(clip * POS, (clip + 1) * POS)
        value = blocks_ref[clip, 0:CHUNK].astype(F32)
        parts = []
        for row, i in PAIRS:
            for col, j in PAIRS:
                phase = 2 * i + j
                part = value[phase * wide : (phase + 1) * wide]
                step = COLS * row + col
                if step != 0:
                    part = pltpu.roll(part, (POS - step) % POS, 1)
                    part = jnp.where(masks[(row, col)], part, 0.0)
                parts.append(part)
        left[:, lanes] = jnp.concatenate(parts, axis=0).astype(BF16)
        for k in range(3):
            right[lanes, k * C1 : (k + 1) * C1] = blocks_ref[
                clip, CHUNK + k * POS : CHUNK + (k + 1) * POS
            ]
    both = jnp.dot(left[...], right[...], preferred_element_type=F32)
    parts = []
    for k in range(3):
        for row in range(3):
            for col in range(3):
                value = None
                for row_pair in PAIRS_OF_TAP[row]:
                    for col_pair in PAIRS_OF_TAP[col]:
                        at = (4 * PAIRS.index(row_pair) + PAIRS.index(col_pair)) * wide
                        piece = both[at : at + wide, k * C1 : (k + 1) * C1]
                        value = piece if value is None else value + piece
                parts.append(value)
    parts.append(jnp.zeros((6 * 128 - 27 * wide, C1), F32))
    turned = jnp.concatenate(parts, axis=0).T
    for block in range(16):
        two = turned[block * thin : (block + 1) * thin]
        out_ref[block] = jnp.concatenate(
            [two[:, 128 * n : 128 * (n + 1)] for n in range(6)], axis=0
        ).astype(out_ref.dtype)


def first_grads(packed_ref, gz_ref, out_ref, moved):
    width, thin = D // 16, C1 // 16
    zeros = jnp.zeros((9 * width, POS), BF16)
    moved[:, 0:POS] = zeros
    moved[:, 17 * POS :] = zeros
    for frame in range(16):
        value = packed_ref[frame, CHUNK:].astype(F32)
        parts = []
        for row, col in TAPS9:
            part = value
            step = COLS * (row - 1) + col - 1
            if step != 0:
                part = pltpu.roll(value, (POS - step) % POS, 1)
                part = jnp.where(spot_mask(row - 1, col - 1, (1, POS), 1), part, 0.0)
            parts.append(part)
        moved[:, (frame + 1) * POS : (frame + 2) * POS] = jnp.concatenate(parts, axis=0).astype(
            BF16
        )
    right = gz_ref[...].reshape(16 * POS, C1)
    parts = []
    for k in range(3):
        parts.append(
            jnp.dot(moved[:, k * POS : (k + 16) * POS], right, preferred_element_type=F32)
        )
    parts.append(jnp.zeros((8 * 128 - 27 * width, C1), F32))
    turned = jnp.concatenate(parts, axis=0).T
    for block in range(16):
        one = turned[block * thin : (block + 1) * thin]
        out_ref[block] = jnp.concatenate(
            [one[:, 128 * n : 128 * (n + 1)] for n in range(8)], axis=0
        ).astype(out_ref.dtype)


def summed(parts_ref, out_ref):
    total = parts_ref[0].astype(F32)
    for source in range(1, 16):
        total = total + parts_ref[source].astype(F32)
    _, rows, width = out_ref.shape
    total = jnp.concatenate(
        [total[rows * n : rows * (n + 1)] for n in range(total.shape[0] // rows)], axis=1
    )
    for k in range(27):
        out_ref[k] = total[:, k * width : (k + 1) * width]


def exchange(value, axis):
    return lax.all_to_all(value, axis, split_axis=0, concat_axis=0, tiled=True)


def with_pair(value):
    return lax.ppermute(value, "seq", [(i, i ^ 1) for i in range(16)])


def with_cross(value):
    swaps = [(i, i + 1) for i in range(1, 15, 2)]
    return lax.ppermute(value, "seq", swaps + [(j, i) for i, j in swaps])


def per_device(tokens, conv_first, bias_first, conv_second, bias_second, pixels, mask_index):
    gelu_tanh = partial(jax.nn.gelu, approximate=True)
    place = (lax.axis_index("seq") % 2).reshape(1).astype(jnp.int32)
    field = tokens.reshape(POS, D)
    packed = call(
        packed_inputs, struct((16, CHUNK + D // 16, POS), BF16), spots(VMEM, VMEM)
    )(pixels.reshape(16, 8, 4 * CO), field)
    packed = exchange(packed, "seq")

    plane = struct((POS, C1), F32)
    pair, keep, cross = call(
        first_conv,
        (plane, plane, plane),
        spots(SMEM, VMEM, VMEM),
        [pltpu.VMEM((POS + 2 * PAD, D), F32)],
    )(place, field, conv_first)
    zsum = with_pair(pair) + keep + with_cross(cross) + bias_first
    hidden = gelu_tanh(zsum).astype(BF16)

    blocks, pair, keep, cross = call(
        loss_and_back,
        (struct((16, CHUNK + 3 * POS, POS), BF16), plane, plane, plane),
        spots(SMEM, *[VMEM] * 7),
        [
            pltpu.VMEM((POS + 2 * PAD, 3 * C1), F32),
            pltpu.VMEM((9, POS, 3 * C1), BF16),
            pltpu.VMEM((4 * POS, CO), BF16),
            pltpu.VMEM((9, POS + 2 * PAD, 3 * C1), F32),
        ],
    )(
        place, with_pair(hidden), hidden, with_cross(hidden), conv_second, bias_second[None],
        packed, mask_index,
    )
    blocks = exchange(blocks, "dp")
    grad_hidden = with_pair(pair) + keep + with_cross(cross)
    grad_z = jax.vjp(gelu_tanh, zsum)[1](grad_hidden)[0].astype(BF16)
    grad_z = lax.all_gather(grad_z, "seq")

    first = call(
        first_grads,
        struct((16, 64, 128), BF16),
        spots(VMEM, VMEM),
        [pltpu.VMEM((9 * D // 16, 18 * POS), BF16)],
    )(packed, grad_z)
    second = call(
        second_grads,
        struct((16, 48, 128), BF16),
        spots(VMEM),
        [pltpu.VMEM((CO, 16 * POS), BF16), pltpu.VMEM((16 * POS, CO), BF16)],
    )(blocks)
    grad_first = call(summed, struct((27, C1 // 16, D // 16), F32), spots(VMEM))(
        exchange(first, "dp")
    )
    grad_second = call(summed, struct((27, C1 // 16, CO // 16), F32), spots(VMEM))(
        exchange(second, "seq")
    )
    return grad_first.transpose(0, 2, 1), grad_second


def solution(mesh):
    return jax.shard_map(
        per_device,
        mesh=mesh,
        in_specs=(
            P("dp", "seq", None, None, None),
            P(),
            P(),
            P(),
            P(),
            P("dp", None, "seq", None, None),
            P("dp", None),
        ),
        out_specs=(P(None, "seq", "dp"), P(None, "seq", "dp")),
        check_vma=False,
    )
```

```python
from functools import partial

import jax
import jax.numpy as jnp
from jax import lax
from jax.experimental import pallas as pl
from jax.experimental.pallas import tpu as pltpu
from jax.sharding import PartitionSpec as P

F32 = jnp.float32
BF16 = jnp.bfloat16
POS, COLS, PAD = 128, 4, 8
D, C1, CO = 512, 128, 384
CHUNK = 4 * CO // 16
FLOPS = 40_000_000_000
TAPS9 = [(row, col) for row in range(3) for col in range(3)]
PHASES = [(i, j) for i in range(2) for j in range(2)]
PAIRS = [(-1, 1), (0, 0), (0, 1), (1, 0)]
PAIRS_OF_TAP = [[(0, 1), (1, 0)], [(0, 0), (0, 1)], [(-1, 1), (0, 0)]]


def token_step(phase, tap):
    return (phase + tap - 1) // 2


def column_mask(step, shape, axis):
    column = lax.broadcasted_iota(jnp.int32, shape, axis) % COLS + step
    return (column >= 0) & (column < COLS)


def spot_mask(row_step, col_step, shape, axis):
    spot = lax.broadcasted_iota(jnp.int32, shape, axis)
    column = spot % COLS + col_step
    row = spot // COLS + row_step
    return (column >= 0) & (column < COLS) & (row >= 0) & (row < POS // COLS)


def call(body, out_shape, in_specs, scratch=(), flops=0, size=0, limit=16, **options):
    return pl.pallas_call(
        body,
        out_shape=out_shape,
        in_specs=in_specs,
        **options,
        scratch_shapes=list(scratch),
        compiler_params=pltpu.CompilerParams(vmem_limit_bytes=limit << 20),
        cost_estimate=pl.CostEstimate(flops=flops, bytes_accessed=size, transcendentals=0),
    )


def struct(shape, dtype):
    return jax.ShapeDtypeStruct(shape, dtype)


SMEM, VMEM, HBM = pltpu.SMEM, pltpu.VMEM, pltpu.HBM


def spots(*kinds):
    return [pl.BlockSpec(memory_space=kind) for kind in kinds]


def packed_inputs(pixel_ref, tokens_ref, out_ref):
    turned = tokens_ref[...].T
    width = D // 16
    for block in range(16):
        pix = pixel_ref[block].astype(F32)
        out_ref[block, 0:CHUNK] = jnp.concatenate(
            [pix[:, n * 128 : (n + 1) * 128] for n in range(4 * CO // 128)], axis=0
        ).astype(BF16)
        out_ref[block, CHUNK:] = turned[block * width : (block + 1) * width]


def first_conv(place_ref, tokens_ref, weight_ref, pair_ref, keep_ref, cross_ref, padded):
    padded[0:PAD] = jnp.zeros((PAD, D), F32)
    padded[PAD + POS :] = jnp.zeros((PAD, D), F32)
    padded[PAD : PAD + POS] = tokens_ref[...].astype(F32)
    total = jnp.zeros((POS, 3 * C1), F32)
    for row, col in TAPS9:
        step = PAD + COLS * (row - 1) + col - 1
        window = padded[step : step + POS]
        if col != 1:
            window = jnp.where(column_mask(col - 1, (POS, D), 0), window, 0.0)
        tap = 3 * row + col
        weight = jnp.concatenate([weight_ref[tap + 9 * k] for k in range(3)], axis=1)
        total = total + jnp.dot(window.astype(BF16), weight, preferred_element_type=F32)
    to_next, to_last = total[:, 0:C1], total[:, 2 * C1 :]
    even = place_ref[0] == 0
    pair_ref[...] = jnp.where(even, to_next, to_last)
    keep_ref[...] = total[:, C1 : 2 * C1]
    cross_ref[...] = jnp.where(even, to_last, to_next)


def tap_weight(weight_ref, row, col):
    return jnp.concatenate([weight_ref[9 * k + 3 * row + col] for k in range(3)], axis=0)


def loss_and_back(place_ref, pair_ref, here_ref, cross_ref, weight_ref, bias_ref, packed_ref,
                  index_ref, blocks_ref, to_pair_ref, keep_ref, to_cross_ref,
                  padded, moved, cots, shifted):
    even = place_ref[0] == 0
    zeros = jnp.zeros((PAD, 3 * C1), F32)
    padded[0:PAD] = zeros
    padded[PAD + POS :] = zeros
    pair, cross = pair_ref[...].astype(F32), cross_ref[...].astype(F32)
    frames = (jnp.where(even, cross, pair), here_ref[...].astype(F32), jnp.where(even, pair, cross))
    for k, value in enumerate(frames):
        padded[PAD : PAD + POS, k * C1 : (k + 1) * C1] = value
        narrow = value.astype(BF16)
        for block in range(16):
            blocks_ref[block, CHUNK + k * POS : CHUNK + (k + 1) * POS] = narrow
    for row, col in TAPS9:
        step = PAD + COLS * (row - 1) + col - 1
        window = padded[step : step + POS]
        if col != 1:
            window = jnp.where(column_mask(col - 1, (POS, 3 * C1), 0), window, 0.0)
        moved[3 * row + col] = window.astype(BF16)
    slabs = []
    for slab in range(16):
        part = packed_ref[slab, 0:CHUNK].astype(F32)
        slabs.append(
            jnp.concatenate([part[8 * n : 8 * n + 8] for n in range(4 * CO // 128)], axis=1)
        )
    pix = jnp.concatenate(slabs, axis=0)
    center = pix - jnp.mean(pix, axis=-1, keepdims=True)
    spread = jnp.mean(center * center, axis=-1, keepdims=True)
    normed = center * lax.rsqrt(spread + 1e-06)
    spot = lax.broadcasted_iota(jnp.int32, (POS, index_ref.shape[1]), 0)
    hits = jnp.sum((spot == index_ref[...]).astype(F32), axis=1, keepdims=True)
    scale = (2.0 / (4 * CO)) * hits
    predict = jnp.zeros((4 * POS, CO), F32)
    for row, col in TAPS9:
        lhs = jnp.concatenate(
            [moved[3 * (token_step(i, row) + 1) + token_step(j, col) + 1] for i, j in PHASES], axis=0
        )
        predict = predict + jnp.dot(
            lhs, tap_weight(weight_ref, row, col), preferred_element_type=F32
        )
    predict = predict + bias_ref[...]
    turned = []
    for k in range(4):
        cot = scale * (predict[k * POS : (k + 1) * POS] - normed[:, k * CO : (k + 1) * CO])
        cot = cot.astype(BF16)
        cots[k * POS : (k + 1) * POS] = cot
        turned.append(cot.astype(F32).T)
    width = CO // 16
    for block in range(16):
        blocks_ref[block, 0:CHUNK] = jnp.concatenate(
            [part[block * width : (block + 1) * width] for part in turned], axis=0
        ).astype(BF16)
    cot = cots[...]
    sums = {}
    for row, col in TAPS9:
        part = lax.dot_general(
            cot, tap_weight(weight_ref, row, col), (((1,), (1,)), ((), ())),
            preferred_element_type=F32,
        )
        for k, (i, j) in enumerate(PHASES):
            key = (token_step(i, row), token_step(j, col))
            piece = part[k * POS : (k + 1) * POS]
            sums[key] = sums[key] + piece if key in sums else piece
    total = sums[(0, 0)]
    for k, ((row, col), value) in enumerate(sums.items()):
        if (row, col) == (0, 0):
            continue
        if col != 0:
            value = jnp.where(column_mask(col, (POS, 3 * C1), 0), value, 0.0)
        shifted[k, 0:PAD] = zeros
        shifted[k, PAD + POS :] = zeros
        shifted[k, PAD : PAD + POS] = value
        step = PAD - COLS * row - col
        total = total + shifted[k, step : step + POS]
    to_last, to_next = total[:, 0:C1], total[:, 2 * C1 :]
    to_pair_ref[...] = jnp.where(even, to_next, to_last)
    keep_ref[...] = total[:, C1 : 2 * C1]
    to_cross_ref[...] = jnp.where(even, to_last, to_next)


def halved(pairs, bit, keep_ref, send_ref):
    for at, (zero, one) in enumerate(pairs):
        keep_ref[at] = jnp.where(bit == 0, zero, one)
        send_ref[at] = jnp.where(bit == 0, one, zero)


def hidden_grads(pair_ref, keep_ref, cross_ref, zsum_ref, out_ref):
    grad = pair_ref[...] + keep_ref[...] + cross_ref[...]
    gelu_tanh = partial(jax.nn.gelu, approximate=True)
    out_ref[...] = jax.vjp(gelu_tanh, zsum_ref[...])[1](grad)[0].astype(BF16)


def second_grads(place_ref, blocks_ref, after_ref, keep_ref, send_ref, left, right):
    del after_ref
    wide, thin = CO // 16, C1 // 16
    masks = {}
    for row in (-1, 0, 1):
        for col in (-1, 0, 1):
            masks[(row, col)] = spot_mask(row, col, (1, POS), 1)
    for clip in range(16):
        lanes = slice(clip * POS, (clip + 1) * POS)
        value = blocks_ref[clip, 0:CHUNK].astype(F32)
        parts = []
        for row, i in PAIRS:
            for col, j in PAIRS:
                phase = 2 * i + j
                part = value[phase * wide : (phase + 1) * wide]
                step = COLS * row + col
                if step != 0:
                    part = pltpu.roll(part, (POS - step) % POS, 1)
                    part = jnp.where(masks[(row, col)], part, 0.0)
                parts.append(part)
        left[:, lanes] = jnp.concatenate(parts, axis=0).astype(BF16)
        for k in range(3):
            right[lanes, k * C1 : (k + 1) * C1] = blocks_ref[
                clip, CHUNK + k * POS : CHUNK + (k + 1) * POS
            ]
    both = jnp.dot(left[...], right[...], preferred_element_type=F32)
    parts = []
    for k in range(3):
        for row in range(3):
            for col in range(3):
                value = None
                for row_pair in PAIRS_OF_TAP[row]:
                    for col_pair in PAIRS_OF_TAP[col]:
                        at = (4 * PAIRS.index(row_pair) + PAIRS.index(col_pair)) * wide
                        piece = both[at : at + wide, k * C1 : (k + 1) * C1]
                        value = piece if value is None else value + piece
                parts.append(value)
    parts.append(jnp.zeros((6 * 128 - 27 * wide, C1), F32))
    turned = jnp.concatenate(parts, axis=0).T
    blocks = [turned[block * thin : (block + 1) * thin] for block in range(16)]
    halved(zip(blocks[0::2], blocks[1::2]), place_ref[0], keep_ref, send_ref)


def half_sum(level, place_ref, kept_ref, came_ref, keep_ref, send_ref):
    pairs = [
        tuple(kept_ref[at] + came_ref[at] for at in (two, two + 1))
        for two in range(0, kept_ref.shape[0], 2)
    ]
    halved(pairs, place_ref[level], keep_ref, send_ref)


def last_sum(kept_ref, came_ref, out_ref):
    total = kept_ref[0] + came_ref[0]
    width = out_ref.shape[2]
    for k in range(27):
        out_ref[k] = total[:, k * width : (k + 1) * width]


def first_grads(packed_ref, gz_ref, out_ref, moved):
    width, thin = D // 16, C1 // 16
    zeros = jnp.zeros((9 * width, POS), BF16)
    moved[:, 0:POS] = zeros
    moved[:, 17 * POS :] = zeros
    for frame in range(16):
        value = packed_ref[frame, CHUNK:].astype(F32)
        parts = []
        for row, col in TAPS9:
            part = value
            step = COLS * (row - 1) + col - 1
            if step != 0:
                part = pltpu.roll(value, (POS - step) % POS, 1)
                part = jnp.where(spot_mask(row - 1, col - 1, (1, POS), 1), part, 0.0)
            parts.append(part)
        moved[:, (frame + 1) * POS : (frame + 2) * POS] = jnp.concatenate(parts, axis=0).astype(
            BF16
        )
    right = gz_ref[...].reshape(16 * POS, C1)
    parts = []
    for k in range(3):
        parts.append(
            jnp.dot(moved[:, k * POS : (k + 16) * POS], right, preferred_element_type=F32)
        )
    parts.append(jnp.zeros((8 * 128 - 27 * width, C1), F32))
    turned = jnp.concatenate(parts, axis=0).T
    for block in range(16):
        one = turned[block * thin : (block + 1) * thin]
        out_ref[block] = jnp.concatenate(
            [one[:, 128 * n : 128 * (n + 1)] for n in range(8)], axis=0
        ).astype(out_ref.dtype)


def summed(parts_ref, out_ref):
    total = parts_ref[0].astype(F32)
    for source in range(1, 16):
        total = total + parts_ref[source].astype(F32)
    _, rows, width = out_ref.shape
    total = jnp.concatenate(
        [total[rows * n : rows * (n + 1)] for n in range(total.shape[0] // rows)], axis=1
    )
    for k in range(27):
        out_ref[k] = total[:, k * width : (k + 1) * width]


def exchange(value, axis):
    return lax.all_to_all(value, axis, split_axis=0, concat_axis=0, tiled=True)


def swapped(value, step):
    return lax.ppermute(value, "seq", [(i, i ^ step) for i in range(16)])


def with_pair(value):
    return swapped(value, 1)


def with_cross(value):
    swaps = [(i, i + 1) for i in range(1, 15, 2)]
    return lax.ppermute(value, "seq", swaps + [(j, i) for i, j in swaps])


def per_device(tokens, conv_first, bias_first, conv_second, bias_second, pixels, mask_index):
    gelu_tanh = partial(jax.nn.gelu, approximate=True)
    place = (lax.axis_index("seq") // jnp.array([1, 2, 4, 8])) % 2
    field = tokens.reshape(POS, D)
    packed = call(
        packed_inputs, struct((16, CHUNK + D // 16, POS), BF16), spots(VMEM, VMEM)
    )(pixels.reshape(16, 8, 4 * CO), field)
    packed = exchange(packed, "seq")

    plane = struct((POS, C1), F32)
    pair, keep, cross = call(
        first_conv,
        (plane, plane, plane),
        spots(SMEM, VMEM, VMEM),
        [pltpu.VMEM((POS + 2 * PAD, D), F32)],
    )(place, field, conv_first)
    zsum = with_pair(pair) + keep + with_cross(cross) + bias_first
    hidden = gelu_tanh(zsum).astype(BF16)

    blocks, pair, keep, cross = call(
        loss_and_back,
        (struct((16, CHUNK + 3 * POS, POS), BF16), plane, plane, plane),
        spots(SMEM, *[VMEM] * 7),
        [
            pltpu.VMEM((POS + 2 * PAD, 3 * C1), F32),
            pltpu.VMEM((9, POS, 3 * C1), BF16),
            pltpu.VMEM((4 * POS, CO), BF16),
            pltpu.VMEM((9, POS + 2 * PAD, 3 * C1), F32),
        ],
    )(
        place, with_pair(hidden), hidden, with_cross(hidden), conv_second, bias_second[None],
        packed, mask_index,
    )
    blocks = exchange(blocks, "dp")
    grad_z = call(hidden_grads, struct((POS, C1), BF16), spots(*[VMEM] * 4), flops=FLOPS)(
        with_pair(pair), keep, with_cross(cross), zsum
    )
    grad_z = lax.all_gather(grad_z, "seq")

    first = call(
        first_grads,
        struct((16, 64, 128), BF16),
        spots(VMEM, VMEM),
        [pltpu.VMEM((9 * D // 16, 18 * POS), BF16)],
    )(packed, grad_z)
    half = struct((8, C1 // 16, 6 * 128), F32)
    keep, send = call(
        second_grads,
        (half, half),
        spots(SMEM, VMEM, pl.ANY),
        [pltpu.VMEM((CO, 16 * POS), BF16), pltpu.VMEM((16 * POS, CO), BF16)],
    )(place, blocks, grad_z)
    for level in (1, 2, 3):
        half = struct((8 >> level, C1 // 16, 6 * 128), F32)
        came = swapped(send, 1 << (level - 1))
        keep, send = call(
            partial(half_sum, level), (half, half), spots(SMEM, VMEM, VMEM)
        )(place, keep, came)
    grad_second = call(last_sum, struct((27, C1 // 16, CO // 16), F32), spots(VMEM, VMEM))(
        keep, swapped(send, 8)
    )
    grad_first = call(summed, struct((27, C1 // 16, D // 16), F32), spots(VMEM))(
        exchange(first, "dp")
    )
    return grad_first.transpose(0, 2, 1), grad_second


def solution(mesh):
    return jax.shard_map(
        per_device,
        mesh=mesh,
        in_specs=(
            P("dp", "seq", None, None, None),
            P(),
            P(),
            P(),
            P(),
            P("dp", None, "seq", None, None),
            P("dp", None),
        ),
        out_specs=(P(None, "seq", "dp"), P(None, "seq", "dp")),
        check_vma=False,
    )
```

```python
from functools import partial

import jax
import jax.numpy as jnp
from jax import lax
from jax.experimental import pallas as pl
from jax.experimental.pallas import tpu as pltpu
from jax.sharding import PartitionSpec as P

F32 = jnp.float32
BF16 = jnp.bfloat16
POS, COLS, PAD = 128, 4, 8
D, C1, CO = 512, 128, 384
CHUNK = 4 * CO // 16
TAPS9 = [(row, col) for row in range(3) for col in range(3)]
PHASES = [(i, j) for i in range(2) for j in range(2)]
PAIRS = [(-1, 1), (0, 0), (0, 1), (1, 0)]
PAIRS_OF_TAP = [[(0, 1), (1, 0)], [(0, 0), (0, 1)], [(-1, 1), (0, 0)]]


def token_step(phase, tap):
    return (phase + tap - 1) // 2


def column_mask(step, shape, axis):
    column = lax.broadcasted_iota(jnp.int32, shape, axis) % COLS + step
    return (column >= 0) & (column < COLS)


def spot_mask(row_step, col_step, shape, axis):
    spot = lax.broadcasted_iota(jnp.int32, shape, axis)
    column = spot % COLS + col_step
    row = spot // COLS + row_step
    return (column >= 0) & (column < COLS) & (row >= 0) & (row < POS // COLS)


def call(body, out_shape, in_specs, scratch=(), flops=0, size=0, limit=16, **options):
    return pl.pallas_call(
        body,
        out_shape=out_shape,
        in_specs=in_specs,
        **options,
        scratch_shapes=list(scratch),
        compiler_params=pltpu.CompilerParams(vmem_limit_bytes=limit << 20),
        cost_estimate=pl.CostEstimate(flops=flops, bytes_accessed=size, transcendentals=0),
    )


def struct(shape, dtype):
    return jax.ShapeDtypeStruct(shape, dtype)


SMEM, VMEM, HBM = pltpu.SMEM, pltpu.VMEM, pltpu.HBM


def spots(*kinds):
    return [pl.BlockSpec(memory_space=kind) for kind in kinds]


def packed_inputs(pixel_ref, tokens_ref, out_ref):
    turned = tokens_ref[...].T
    width = D // 16
    for block in range(16):
        pix = pixel_ref[block].astype(F32)
        out_ref[block, 0:CHUNK] = jnp.concatenate(
            [pix[:, n * 128 : (n + 1) * 128] for n in range(4 * CO // 128)], axis=0
        ).astype(BF16)
        out_ref[block, CHUNK:] = turned[block * width : (block + 1) * width]


def first_conv(place_ref, tokens_ref, weight_ref, pair_ref, keep_ref, cross_ref, padded):
    padded[0:PAD] = jnp.zeros((PAD, D), F32)
    padded[PAD + POS :] = jnp.zeros((PAD, D), F32)
    padded[PAD : PAD + POS] = tokens_ref[...].astype(F32)
    total = jnp.zeros((POS, 3 * C1), F32)
    for row, col in TAPS9:
        step = PAD + COLS * (row - 1) + col - 1
        window = padded[step : step + POS]
        if col != 1:
            window = jnp.where(column_mask(col - 1, (POS, D), 0), window, 0.0)
        tap = 3 * row + col
        weight = jnp.concatenate([weight_ref[tap + 9 * k] for k in range(3)], axis=1)
        total = total + jnp.dot(window.astype(BF16), weight, preferred_element_type=F32)
    to_next, to_last = total[:, 0:C1], total[:, 2 * C1 :]
    even = place_ref[0] == 0
    pair_ref[...] = jnp.where(even, to_next, to_last)
    keep_ref[...] = total[:, C1 : 2 * C1]
    cross_ref[...] = jnp.where(even, to_last, to_next)


def tap_weight(weight_ref, row, col):
    return jnp.concatenate([weight_ref[9 * k + 3 * row + col] for k in range(3)], axis=0)


def loss_cotangent(place_ref, pair_ref, here_ref, cross_ref, weight_ref, bias_ref, packed_ref,
                   index_ref, blocks_ref, cots, padded, moved):
    even = place_ref[0] == 0
    zeros = jnp.zeros((PAD, 3 * C1), F32)
    padded[0:PAD] = zeros
    padded[PAD + POS :] = zeros
    pair, cross = pair_ref[...].astype(F32), cross_ref[...].astype(F32)
    frames = (jnp.where(even, cross, pair), here_ref[...].astype(F32), jnp.where(even, pair, cross))
    for k, value in enumerate(frames):
        padded[PAD : PAD + POS, k * C1 : (k + 1) * C1] = value
        narrow = value.astype(BF16)
        for block in range(16):
            blocks_ref[block, CHUNK + k * POS : CHUNK + (k + 1) * POS] = narrow
    for row, col in TAPS9:
        step = PAD + COLS * (row - 1) + col - 1
        window = padded[step : step + POS]
        if col != 1:
            window = jnp.where(column_mask(col - 1, (POS, 3 * C1), 0), window, 0.0)
        moved[3 * row + col] = window.astype(BF16)
    slabs = []
    for slab in range(16):
        part = packed_ref[slab, 0:CHUNK].astype(F32)
        slabs.append(
            jnp.concatenate([part[8 * n : 8 * n + 8] for n in range(4 * CO // 128)], axis=1)
        )
    pix = jnp.concatenate(slabs, axis=0)
    center = pix - jnp.mean(pix, axis=-1, keepdims=True)
    spread = jnp.mean(center * center, axis=-1, keepdims=True)
    normed = center * lax.rsqrt(spread + 1e-06)
    spot = lax.broadcasted_iota(jnp.int32, (POS, index_ref.shape[1]), 0)
    hits = jnp.sum((spot == index_ref[...]).astype(F32), axis=1, keepdims=True)
    scale = (2.0 / (4 * CO)) * hits
    predict = jnp.zeros((4 * POS, CO), F32)
    for row, col in TAPS9:
        lhs = jnp.concatenate(
            [moved[3 * (token_step(i, row) + 1) + token_step(j, col) + 1] for i, j in PHASES], axis=0
        )
        predict = predict + jnp.dot(
            lhs, tap_weight(weight_ref, row, col), preferred_element_type=F32
        )
    predict = predict + bias_ref[...]
    turned = []
    for k in range(4):
        cot = scale * (predict[k * POS : (k + 1) * POS] - normed[:, k * CO : (k + 1) * CO])
        cot = cot.astype(BF16)
        cots[k * POS : (k + 1) * POS] = cot
        turned.append(cot.astype(F32).T)
    width = CO // 16
    for block in range(16):
        blocks_ref[block, 0:CHUNK] = jnp.concatenate(
            [part[block * width : (block + 1) * width] for part in turned], axis=0
        ).astype(BF16)

def back_conv(place_ref, cots, weight_ref, to_pair_ref, keep_ref, to_cross_ref, shifted):
    even = place_ref[0] == 0
    zeros = jnp.zeros((PAD, 3 * C1), F32)
    cot = cots[...]
    sums = {}
    for row, col in TAPS9:
        part = lax.dot_general(
            cot, tap_weight(weight_ref, row, col), (((1,), (1,)), ((), ())),
            preferred_element_type=F32,
        )
        for k, (i, j) in enumerate(PHASES):
            key = (token_step(i, row), token_step(j, col))
            piece = part[k * POS : (k + 1) * POS]
            sums[key] = sums[key] + piece if key in sums else piece
    total = sums[(0, 0)]
    for k, ((row, col), value) in enumerate(sums.items()):
        if (row, col) == (0, 0):
            continue
        if col != 0:
            value = jnp.where(column_mask(col, (POS, 3 * C1), 0), value, 0.0)
        shifted[k, 0:PAD] = zeros
        shifted[k, PAD + POS :] = zeros
        shifted[k, PAD : PAD + POS] = value
        step = PAD - COLS * row - col
        total = total + shifted[k, step : step + POS]
    to_last, to_next = total[:, 0:C1], total[:, 2 * C1 :]
    to_pair_ref[...] = jnp.where(even, to_next, to_last)
    keep_ref[...] = total[:, C1 : 2 * C1]
    to_cross_ref[...] = jnp.where(even, to_last, to_next)


def halved(pairs, bit, keep_ref, send_ref):
    for at, (zero, one) in enumerate(pairs):
        keep_ref[at] = jnp.where(bit == 0, zero, one)
        send_ref[at] = jnp.where(bit == 0, one, zero)


def hidden_grads(pair_ref, keep_ref, cross_ref, zsum_ref, out_ref):
    grad = pair_ref[...] + keep_ref[...] + cross_ref[...]
    gelu_tanh = partial(jax.nn.gelu, approximate=True)
    out_ref[...] = jax.vjp(gelu_tanh, zsum_ref[...])[1](grad)[0].astype(BF16)


def second_grads(blocks_ref, out_ref, left, right):
    wide, thin = CO // 16, C1 // 16
    masks = {}
    for row in (-1, 0, 1):
        for col in (-1, 0, 1):
            masks[(row, col)] = spot_mask(row, col, (1, POS), 1)
    for clip in range(16):
        lanes = slice(clip * POS, (clip + 1) * POS)
        value = blocks_ref[clip, 0:CHUNK].astype(F32)
        parts = []
        for row, i in PAIRS:
            for col, j in PAIRS:
                phase = 2 * i + j
                part = value[phase * wide : (phase + 1) * wide]
                step = COLS * row + col
                if step != 0:
                    part = pltpu.roll(part, (POS - step) % POS, 1)
                    part = jnp.where(masks[(row, col)], part, 0.0)
                parts.append(part)
        left[:, lanes] = jnp.concatenate(parts, axis=0).astype(BF16)
        for k in range(3):
            right[lanes, k * C1 : (k + 1) * C1] = blocks_ref[
                clip, CHUNK + k * POS : CHUNK + (k + 1) * POS
            ]
    both = jnp.dot(left[...], right[...], preferred_element_type=F32)
    parts = []
    for k in range(3):
        for row in range(3):
            for col in range(3):
                value = None
                for row_pair in PAIRS_OF_TAP[row]:
                    for col_pair in PAIRS_OF_TAP[col]:
                        at = (4 * PAIRS.index(row_pair) + PAIRS.index(col_pair)) * wide
                        piece = both[at : at + wide, k * C1 : (k + 1) * C1]
                        value = piece if value is None else value + piece
                parts.append(value)
    parts.append(jnp.zeros((6 * 128 - 27 * wide, C1), F32))
    turned = jnp.concatenate(parts, axis=0).T
    for block in range(16):
        two = turned[block * thin : (block + 1) * thin]
        out_ref[block] = jnp.concatenate(
            [two[:, 128 * n : 128 * (n + 1)] for n in range(6)], axis=0
        ).astype(out_ref.dtype)


def half_sum(level, place_ref, kept_ref, came_ref, keep_ref, send_ref):
    pairs = [
        tuple(kept_ref[at] + came_ref[at] for at in (two, two + 1))
        for two in range(0, kept_ref.shape[0], 2)
    ]
    halved(pairs, place_ref[level], keep_ref, send_ref)


def last_sum(kept_ref, came_ref, out_ref):
    total = kept_ref[0] + came_ref[0]
    width = out_ref.shape[2]
    for k in range(27):
        out_ref[k] = total[:, k * width : (k + 1) * width]


def first_grads(place_ref, packed_ref, gz_ref, keep_ref, send_ref, moved):
    width, thin = D // 16, C1 // 16
    zeros = jnp.zeros((9 * width, POS), BF16)
    moved[:, 0:POS] = zeros
    moved[:, 17 * POS :] = zeros
    for frame in range(16):
        value = packed_ref[frame, CHUNK:].astype(F32)
        parts = []
        for row, col in TAPS9:
            part = value
            step = COLS * (row - 1) + col - 1
            if step != 0:
                part = pltpu.roll(value, (POS - step) % POS, 1)
                part = jnp.where(spot_mask(row - 1, col - 1, (1, POS), 1), part, 0.0)
            parts.append(part)
        moved[:, (frame + 1) * POS : (frame + 2) * POS] = jnp.concatenate(parts, axis=0).astype(
            BF16
        )
    right = gz_ref[...].reshape(16 * POS, C1)
    parts = []
    for k in range(3):
        parts.append(
            jnp.dot(moved[:, k * POS : (k + 16) * POS], right, preferred_element_type=F32)
        )
    parts.append(jnp.zeros((7 * 128 - 27 * width, C1), F32))
    turned = jnp.concatenate(parts, axis=0).T
    blocks = [turned[block * thin : (block + 1) * thin] for block in range(16)]
    halved(zip(blocks[0::2], blocks[1::2]), place_ref[1], keep_ref, send_ref)


def summed(parts_ref, out_ref):
    total = parts_ref[0].astype(F32)
    for source in range(1, 16):
        total = total + parts_ref[source].astype(F32)
    _, rows, width = out_ref.shape
    total = jnp.concatenate(
        [total[rows * n : rows * (n + 1)] for n in range(total.shape[0] // rows)], axis=1
    )
    for k in range(27):
        out_ref[k] = total[:, k * width : (k + 1) * width]


def exchange(value, axis):
    return lax.all_to_all(value, axis, split_axis=0, concat_axis=0, tiled=True)


def swapped(value, step, axis="seq"):
    return lax.ppermute(value, axis, [(i, i ^ step) for i in range(16)])


def with_pair(value):
    return swapped(value, 1)


def with_cross(value):
    swaps = [(i, i + 1) for i in range(1, 15, 2)]
    return lax.ppermute(value, "seq", swaps + [(j, i) for i, j in swaps])


def per_device(tokens, conv_first, bias_first, conv_second, bias_second, pixels, mask_index):
    gelu_tanh = partial(jax.nn.gelu, approximate=True)
    clip, frame = lax.axis_index("dp"), lax.axis_index("seq")
    place = jnp.stack([frame, clip, clip // 2, clip // 4, clip // 8]) % 2
    field = tokens.reshape(POS, D)
    packed = call(
        packed_inputs, struct((16, CHUNK + D // 16, POS), BF16), spots(VMEM, VMEM)
    )(pixels.reshape(16, 8, 4 * CO), field)
    packed = exchange(packed, "seq")

    plane = struct((POS, C1), F32)
    pair, keep, cross = call(
        first_conv,
        (plane, plane, plane),
        spots(SMEM, VMEM, VMEM),
        [pltpu.VMEM((POS + 2 * PAD, D), F32)],
    )(place, field, conv_first)
    zsum = with_pair(pair) + keep + with_cross(cross) + bias_first
    hidden = gelu_tanh(zsum).astype(BF16)

    blocks, cot = call(
        loss_cotangent,
        (struct((16, CHUNK + 3 * POS, POS), BF16), struct((4 * POS, CO), BF16)),
        spots(SMEM, *[VMEM] * 7),
        [pltpu.VMEM((POS + 2 * PAD, 3 * C1), F32), pltpu.VMEM((9, POS, 3 * C1), BF16)],
    )(
        place, with_pair(hidden), hidden, with_cross(hidden), conv_second, bias_second[None],
        packed, mask_index,
    )
    pair, keep, cross = call(
        back_conv,
        (plane, plane, plane),
        spots(SMEM, VMEM, VMEM),
        [pltpu.VMEM((9, POS + 2 * PAD, 3 * C1), F32)],
    )(place, cot, conv_second)
    blocks = exchange(blocks, "dp")
    grad_z = call(hidden_grads, struct((POS, C1), BF16), spots(*[VMEM] * 4))(
        with_pair(pair), keep, with_cross(cross), zsum
    )
    grad_z = lax.all_gather(grad_z, "seq")

    half = struct((8, C1 // 16, 7 * 128), F32)
    keep, send = call(
        first_grads,
        (half, half),
        spots(SMEM, VMEM, VMEM),
        [pltpu.VMEM((9 * D // 16, 18 * POS), BF16)],
    )(place, packed, grad_z)
    for level in (1, 2, 3):
        half = struct((8 >> level, C1 // 16, 7 * 128), F32)
        came = swapped(send, 1 << (level - 1), "dp")
        keep, send = call(
            partial(half_sum, level + 1), (half, half), spots(SMEM, VMEM, VMEM)
        )(place, keep, came)
    grad_first = call(last_sum, struct((27, C1 // 16, D // 16), F32), spots(VMEM, VMEM))(
        keep, swapped(send, 8, "dp")
    )
    second = call(
        second_grads,
        struct((16, 48, 128), BF16),
        spots(VMEM),
        [pltpu.VMEM((CO, 16 * POS), BF16), pltpu.VMEM((16 * POS, CO), BF16)],
    )(blocks)
    grad_second = call(summed, struct((27, C1 // 16, CO // 16), F32), spots(VMEM))(
        exchange(second, "seq")
    )
    return grad_first.transpose(0, 2, 1), grad_second


def solution(mesh):
    return jax.shard_map(
        per_device,
        mesh=mesh,
        in_specs=(
            P("dp", "seq", None, None, None),
            P(),
            P(),
            P(),
            P(),
            P("dp", None, "seq", None, None),
            P("dp", None),
        ),
        out_specs=(P(None, "seq", "dp"), P(None, "seq", "dp")),
        check_vma=False,
    )
```

```python
from functools import partial

import jax
import jax.numpy as jnp
from jax import lax
from jax.experimental import pallas as pl
from jax.experimental.pallas import tpu as pltpu
from jax.sharding import PartitionSpec as P

F32 = jnp.float32
BF16 = jnp.bfloat16
POS, COLS, PAD = 128, 4, 8
D, C1, CO = 512, 128, 384
CHUNK = 4 * CO // 16
FLOPS = 40_000_000_000
STEPS = (2, 1, 8, 4)
TAPS9 = [(row, col) for row in range(3) for col in range(3)]
PHASES = [(i, j) for i in range(2) for j in range(2)]
PAIRS = [(-1, 1), (0, 0), (0, 1), (1, 0)]
PAIRS_OF_TAP = [[(0, 1), (1, 0)], [(0, 0), (0, 1)], [(-1, 1), (0, 0)]]


def token_step(phase, tap):
    return (phase + tap - 1) // 2


def column_mask(step, shape, axis):
    column = lax.broadcasted_iota(jnp.int32, shape, axis) % COLS + step
    return (column >= 0) & (column < COLS)


def spot_mask(row_step, col_step, shape, axis):
    spot = lax.broadcasted_iota(jnp.int32, shape, axis)
    column = spot % COLS + col_step
    row = spot // COLS + row_step
    return (column >= 0) & (column < COLS) & (row >= 0) & (row < POS // COLS)


def call(body, out_shape, in_specs, scratch=(), flops=0, size=0, limit=16, **options):
    return pl.pallas_call(
        body,
        out_shape=out_shape,
        in_specs=in_specs,
        **options,
        scratch_shapes=list(scratch),
        compiler_params=pltpu.CompilerParams(vmem_limit_bytes=limit << 20),
        cost_estimate=pl.CostEstimate(flops=flops, bytes_accessed=size, transcendentals=0),
    )


def struct(shape, dtype):
    return jax.ShapeDtypeStruct(shape, dtype)


SMEM, VMEM, HBM = pltpu.SMEM, pltpu.VMEM, pltpu.HBM


def spots(*kinds):
    return [pl.BlockSpec(memory_space=kind) for kind in kinds]


def packed_inputs(pixel_ref, tokens_ref, before_ref, out_ref):
    del before_ref
    turned = tokens_ref[...].T
    width = D // 16
    for block in range(16):
        pix = pixel_ref[block].astype(F32)
        out_ref[block, 0:CHUNK] = jnp.concatenate(
            [pix[:, n * 128 : (n + 1) * 128] for n in range(4 * CO // 128)], axis=0
        ).astype(BF16)
        out_ref[block, CHUNK:] = turned[block * width : (block + 1) * width]


def first_conv(place_ref, tokens_ref, weight_ref, pair_ref, keep_ref, cross_ref, padded):
    padded[0:PAD] = jnp.zeros((PAD, D), F32)
    padded[PAD + POS :] = jnp.zeros((PAD, D), F32)
    padded[PAD : PAD + POS] = tokens_ref[...].astype(F32)
    total = jnp.zeros((POS, 3 * C1), F32)
    for row, col in TAPS9:
        step = PAD + COLS * (row - 1) + col - 1
        window = padded[step : step + POS]
        if col != 1:
            window = jnp.where(column_mask(col - 1, (POS, D), 0), window, 0.0)
        tap = 3 * row + col
        weight = jnp.concatenate([weight_ref[tap + 9 * k] for k in range(3)], axis=1)
        total = total + jnp.dot(window.astype(BF16), weight, preferred_element_type=F32)
    to_next, to_last = total[:, 0:C1], total[:, 2 * C1 :]
    even = place_ref[0] == 0
    pair_ref[...] = jnp.where(even, to_next, to_last)
    keep_ref[...] = total[:, C1 : 2 * C1]
    cross_ref[...] = jnp.where(even, to_last, to_next)


def tap_weight(weight_ref, row, col):
    return jnp.concatenate([weight_ref[9 * k + 3 * row + col] for k in range(3)], axis=0)


def loss_cotangent(place_ref, pair_ref, here_ref, cross_ref, weight_ref, bias_ref, packed_ref,
                   index_ref, blocks_ref, cots, padded, moved):
    even = place_ref[0] == 0
    zeros = jnp.zeros((PAD, 3 * C1), F32)
    padded[0:PAD] = zeros
    padded[PAD + POS :] = zeros
    pair, cross = pair_ref[...].astype(F32), cross_ref[...].astype(F32)
    frames = (jnp.where(even, cross, pair), here_ref[...].astype(F32), jnp.where(even, pair, cross))
    for k, value in enumerate(frames):
        padded[PAD : PAD + POS, k * C1 : (k + 1) * C1] = value
        narrow = value.astype(BF16)
        for block in range(16):
            blocks_ref[block, CHUNK + k * POS : CHUNK + (k + 1) * POS] = narrow
    for row, col in TAPS9:
        step = PAD + COLS * (row - 1) + col - 1
        window = padded[step : step + POS]
        if col != 1:
            window = jnp.where(column_mask(col - 1, (POS, 3 * C1), 0), window, 0.0)
        moved[3 * row + col] = window.astype(BF16)
    slabs = []
    for slab in range(16):
        part = packed_ref[slab, 0:CHUNK].astype(F32)
        slabs.append(
            jnp.concatenate([part[8 * n : 8 * n + 8] for n in range(4 * CO // 128)], axis=1)
        )
    pix = jnp.concatenate(slabs, axis=0)
    center = pix - jnp.mean(pix, axis=-1, keepdims=True)
    spread = jnp.mean(center * center, axis=-1, keepdims=True)
    normed = center * lax.rsqrt(spread + 1e-06)
    spot = lax.broadcasted_iota(jnp.int32, (POS, index_ref.shape[1]), 0)
    hits = jnp.sum((spot == index_ref[...]).astype(F32), axis=1, keepdims=True)
    scale = (2.0 / (4 * CO)) * hits
    predict = jnp.zeros((4 * POS, CO), F32)
    for row, col in TAPS9:
        lhs = jnp.concatenate(
            [moved[3 * (token_step(i, row) + 1) + token_step(j, col) + 1] for i, j in PHASES], axis=0
        )
        predict = predict + jnp.dot(
            lhs, tap_weight(weight_ref, row, col), preferred_element_type=F32
        )
    predict = predict + bias_ref[...]
    turned = []
    for k in range(4):
        cot = scale * (predict[k * POS : (k + 1) * POS] - normed[:, k * CO : (k + 1) * CO])
        cot = cot.astype(BF16)
        cots[k * POS : (k + 1) * POS] = cot
        turned.append(cot.astype(F32).T)
    width = CO // 16
    for block in range(16):
        blocks_ref[block, 0:CHUNK] = jnp.concatenate(
            [part[block * width : (block + 1) * width] for part in turned], axis=0
        ).astype(BF16)

def back_conv(place_ref, cots, weight_ref, to_pair_ref, keep_ref, to_cross_ref, shifted):
    even = place_ref[0] == 0
    zeros = jnp.zeros((PAD, 3 * C1), F32)
    cot = cots[...]
    sums = {}
    for row, col in TAPS9:
        part = lax.dot_general(
            cot, tap_weight(weight_ref, row, col), (((1,), (1,)), ((), ())),
            preferred_element_type=F32,
        )
        for k, (i, j) in enumerate(PHASES):
            key = (token_step(i, row), token_step(j, col))
            piece = part[k * POS : (k + 1) * POS]
            sums[key] = sums[key] + piece if key in sums else piece
    total = sums[(0, 0)]
    for k, ((row, col), value) in enumerate(sums.items()):
        if (row, col) == (0, 0):
            continue
        if col != 0:
            value = jnp.where(column_mask(col, (POS, 3 * C1), 0), value, 0.0)
        shifted[k, 0:PAD] = zeros
        shifted[k, PAD + POS :] = zeros
        shifted[k, PAD : PAD + POS] = value
        step = PAD - COLS * row - col
        total = total + shifted[k, step : step + POS]
    to_last, to_next = total[:, 0:C1], total[:, 2 * C1 :]
    to_pair_ref[...] = jnp.where(even, to_next, to_last)
    keep_ref[...] = total[:, C1 : 2 * C1]
    to_cross_ref[...] = jnp.where(even, to_last, to_next)


def halved(pairs, bit, keep_ref, send_ref):
    for at, (zero, one) in enumerate(pairs):
        keep_ref[at] = jnp.where(bit == 0, zero, one)
        send_ref[at] = jnp.where(bit == 0, one, zero)


def hidden_values(pair_ref, keep_ref, cross_ref, bias_ref, zsum_ref, hidden_ref):
    zsum = pair_ref[...] + keep_ref[...] + cross_ref[...] + bias_ref[...]
    zsum_ref[...] = zsum
    hidden_ref[...] = jax.nn.gelu(zsum, approximate=True).astype(BF16)


def hidden_grads(pair_ref, keep_ref, cross_ref, zsum_ref, out_ref):
    grad = pair_ref[...] + keep_ref[...] + cross_ref[...]
    gelu_tanh = partial(jax.nn.gelu, approximate=True)
    out_ref[...] = jax.vjp(gelu_tanh, zsum_ref[...])[1](grad)[0].astype(BF16)


def second_grads(blocks_ref, before_ref, out_ref, left, right):
    del before_ref
    wide, thin = CO // 16, C1 // 16
    masks = {}
    for row in (-1, 0, 1):
        for col in (-1, 0, 1):
            masks[(row, col)] = spot_mask(row, col, (1, POS), 1)
    for clip in range(16):
        lanes = slice(clip * POS, (clip + 1) * POS)
        value = blocks_ref[clip, 0:CHUNK].astype(F32)
        parts = []
        for row, i in PAIRS:
            for col, j in PAIRS:
                phase = 2 * i + j
                part = value[phase * wide : (phase + 1) * wide]
                step = COLS * row + col
                if step != 0:
                    part = pltpu.roll(part, (POS - step) % POS, 1)
                    part = jnp.where(masks[(row, col)], part, 0.0)
                parts.append(part)
        left[:, lanes] = jnp.concatenate(parts, axis=0).astype(BF16)
        for k in range(3):
            right[lanes, k * C1 : (k + 1) * C1] = blocks_ref[
                clip, CHUNK + k * POS : CHUNK + (k + 1) * POS
            ]
    both = jnp.dot(left[...], right[...], preferred_element_type=F32)
    parts = []
    for k in range(3):
        for row in range(3):
            for col in range(3):
                value = None
                for row_pair in PAIRS_OF_TAP[row]:
                    for col_pair in PAIRS_OF_TAP[col]:
                        at = (4 * PAIRS.index(row_pair) + PAIRS.index(col_pair)) * wide
                        piece = both[at : at + wide, k * C1 : (k + 1) * C1]
                        value = piece if value is None else value + piece
                parts.append(value)
    parts.append(jnp.zeros((6 * 128 - 27 * wide, C1), F32))
    turned = jnp.concatenate(parts, axis=0).T
    for block in range(16):
        two = turned[block * thin : (block + 1) * thin]
        out_ref[block] = jnp.concatenate(
            [two[:, 128 * n : 128 * (n + 1)] for n in range(6)], axis=0
        ).astype(out_ref.dtype)


def half_sum(level, place_ref, kept_ref, came_ref, keep_ref, send_ref):
    pairs = [
        tuple(kept_ref[at] + came_ref[at] for at in (two, two + 1))
        for two in range(0, kept_ref.shape[0], 2)
    ]
    halved(pairs, place_ref[level], keep_ref, send_ref)


def last_sum(kept_ref, came_ref, out_ref):
    total = kept_ref[0] + came_ref[0]
    width = out_ref.shape[2]
    for k in range(27):
        out_ref[k] = total[:, k * width : (k + 1) * width]


def first_grads(place_ref, packed_ref, gz_ref, keep_ref, send_ref, moved):
    width, thin = D // 16, C1 // 16
    zeros = jnp.zeros((9 * width, POS), BF16)
    moved[:, 0:POS] = zeros
    moved[:, 17 * POS :] = zeros
    for frame in range(16):
        value = packed_ref[frame, CHUNK:].astype(F32)
        parts = []
        for row, col in TAPS9:
            part = value
            step = COLS * (row - 1) + col - 1
            if step != 0:
                part = pltpu.roll(value, (POS - step) % POS, 1)
                part = jnp.where(spot_mask(row - 1, col - 1, (1, POS), 1), part, 0.0)
            parts.append(part)
        moved[:, (frame + 1) * POS : (frame + 2) * POS] = jnp.concatenate(parts, axis=0).astype(
            BF16
        )
    right = gz_ref[...].reshape(16 * POS, C1)
    parts = []
    for k in range(3):
        parts.append(
            jnp.dot(moved[:, k * POS : (k + 16) * POS], right, preferred_element_type=F32)
        )
    parts.append(jnp.zeros((7 * 128 - 27 * width, C1), F32))
    turned = jnp.concatenate(parts, axis=0).T
    order = [sum(step for n, step in enumerate(STEPS) if slot >> n & 1) for slot in range(16)]
    blocks = [turned[block * thin : (block + 1) * thin] for block in order]
    halved(zip(blocks[0::2], blocks[1::2]), place_ref[1], keep_ref, send_ref)


def summed(parts_ref, out_ref):
    total = parts_ref[0].astype(F32)
    for source in range(1, 16):
        total = total + parts_ref[source].astype(F32)
    _, rows, width = out_ref.shape
    total = jnp.concatenate(
        [total[rows * n : rows * (n + 1)] for n in range(total.shape[0] // rows)], axis=1
    )
    for k in range(27):
        out_ref[k] = total[:, k * width : (k + 1) * width]


def exchange(value, axis):
    return lax.all_to_all(value, axis, split_axis=0, concat_axis=0, tiled=True)


def swapped(value, step, axis="seq"):
    return lax.ppermute(value, axis, [(i, i ^ step) for i in range(16)])


def with_pair(value):
    return swapped(value, 1)


def with_cross(value):
    swaps = [(i, i + 1) for i in range(1, 15, 2)]
    return lax.ppermute(value, "seq", swaps + [(j, i) for i, j in swaps])


def per_device(tokens, conv_first, bias_first, conv_second, bias_second, pixels, mask_index):
    clip, frame = lax.axis_index("dp"), lax.axis_index("seq")
    place = jnp.stack([frame] + [clip // step for step in STEPS]) % 2
    field = tokens.reshape(POS, D)
    plane = struct((POS, C1), F32)
    pair, keep, cross = call(
        first_conv,
        (plane, plane, plane),
        spots(SMEM, VMEM, VMEM),
        [pltpu.VMEM((POS + 2 * PAD, D), F32)],
    )(place, field, conv_first)
    packed = call(
        packed_inputs, struct((16, CHUNK + D // 16, POS), BF16), spots(VMEM, VMEM, pl.ANY)
    )(pixels.reshape(16, 8, 4 * CO), field, keep)
    packed = exchange(packed, "seq")
    zsum, hidden = call(
        hidden_values,
        (plane, struct((POS, C1), BF16)),
        spots(*[VMEM] * 4),
        flops=FLOPS,
    )(with_pair(pair), keep, with_cross(cross), bias_first[None])

    blocks, cot = call(
        loss_cotangent,
        (struct((16, CHUNK + 3 * POS, POS), BF16), struct((4 * POS, CO), BF16)),
        spots(SMEM, *[VMEM] * 7),
        [pltpu.VMEM((POS + 2 * PAD, 3 * C1), F32), pltpu.VMEM((9, POS, 3 * C1), BF16)],
    )(
        place, with_pair(hidden), hidden, with_cross(hidden), conv_second, bias_second[None],
        packed, mask_index,
    )
    pair, keep, cross = call(
        back_conv,
        (plane, plane, plane),
        spots(SMEM, VMEM, VMEM),
        [pltpu.VMEM((9, POS + 2 * PAD, 3 * C1), F32)],
    )(place, cot, conv_second)
    blocks = exchange(blocks, "dp")
    grad_z = call(hidden_grads, struct((POS, C1), BF16), spots(*[VMEM] * 4), flops=FLOPS)(
        with_pair(pair), keep, with_cross(cross), zsum
    )
    grad_z = lax.all_gather(grad_z, "seq")

    half = struct((8, C1 // 16, 7 * 128), F32)
    keep, send = call(
        first_grads,
        (half, half),
        spots(SMEM, VMEM, VMEM),
        [pltpu.VMEM((9 * D // 16, 18 * POS), BF16)],
    )(place, packed, grad_z)
    grad_first_half = keep
    for level in (1, 2, 3):
        half = struct((8 >> level, C1 // 16, 7 * 128), F32)
        came = swapped(send, STEPS[level - 1], "dp")
        keep, send = call(
            partial(half_sum, level + 1), (half, half), spots(SMEM, VMEM, VMEM)
        )(place, keep, came)
    grad_first = call(last_sum, struct((27, C1 // 16, D // 16), F32), spots(VMEM, VMEM))(
        keep, swapped(send, STEPS[3], "dp")
    )
    second = call(
        second_grads,
        struct((16, 48, 128), BF16),
        spots(VMEM, pl.ANY),
        [pltpu.VMEM((CO, 16 * POS), BF16), pltpu.VMEM((16 * POS, CO), BF16)],
    )(blocks, grad_first_half)
    grad_second = call(summed, struct((27, C1 // 16, CO // 16), F32), spots(VMEM))(
        exchange(second, "seq")
    )
    return grad_first.transpose(0, 2, 1), grad_second


def solution(mesh):
    return jax.shard_map(
        per_device,
        mesh=mesh,
        in_specs=(
            P("dp", "seq", None, None, None),
            P(),
            P(),
            P(),
            P(),
            P("dp", None, "seq", None, None),
            P("dp", None),
        ),
        out_specs=(P(None, "seq", "dp"), P(None, "seq", "dp")),
        check_vma=False,
    )
```

```python
from functools import partial

import jax
import jax.numpy as jnp
from jax import lax
from jax.experimental import pallas as pl
from jax.experimental.pallas import tpu as pltpu
from jax.sharding import PartitionSpec as P

F32 = jnp.float32
BF16 = jnp.bfloat16
POS, COLS, PAD = 128, 4, 8
D, C1, CO = 512, 128, 384
CHUNK = 4 * CO // 16
FLOPS = 40_000_000_000
STEPS = (2, 1, 8, 4)
TAPS9 = [(row, col) for row in range(3) for col in range(3)]
PHASES = [(i, j) for i in range(2) for j in range(2)]
PAIRS = [(-1, 1), (0, 0), (0, 1), (1, 0)]
PAIRS_OF_TAP = [[(0, 1), (1, 0)], [(0, 0), (0, 1)], [(-1, 1), (0, 0)]]


def token_step(phase, tap):
    return (phase + tap - 1) // 2


def column_mask(step, shape, axis):
    column = lax.broadcasted_iota(jnp.int32, shape, axis) % COLS + step
    return (column >= 0) & (column < COLS)


def spot_mask(row_step, col_step, shape, axis):
    spot = lax.broadcasted_iota(jnp.int32, shape, axis)
    column = spot % COLS + col_step
    row = spot // COLS + row_step
    return (column >= 0) & (column < COLS) & (row >= 0) & (row < POS // COLS)


def call(body, out_shape, in_specs, scratch=(), flops=0, size=0, limit=16, **options):
    return pl.pallas_call(
        body,
        out_shape=out_shape,
        in_specs=in_specs,
        **options,
        scratch_shapes=list(scratch),
        compiler_params=pltpu.CompilerParams(vmem_limit_bytes=limit << 20),
        cost_estimate=pl.CostEstimate(flops=flops, bytes_accessed=size, transcendentals=0),
    )


def struct(shape, dtype):
    return jax.ShapeDtypeStruct(shape, dtype)


VMEM = pltpu.VMEM


def spots(*kinds):
    return [pl.BlockSpec(memory_space=kind) for kind in kinds]


def packed_inputs(pixel_ref, tokens_ref, out_ref):
    turned = tokens_ref[...].T
    width = D // 16
    for block in range(16):
        pix = pixel_ref[block].astype(F32)
        out_ref[block, 0:CHUNK] = jnp.concatenate(
            [pix[:, n * 128 : (n + 1) * 128] for n in range(4 * CO // 128)], axis=0
        ).astype(BF16)
        out_ref[block, CHUNK:] = turned[block * width : (block + 1) * width]


def first_conv(tokens_ref, weight_ref, before_ref, pair_ref, keep_ref, cross_ref, padded):
    del before_ref
    padded[0:PAD] = jnp.zeros((PAD, D), F32)
    padded[PAD + POS :] = jnp.zeros((PAD, D), F32)
    padded[PAD : PAD + POS] = tokens_ref[...].astype(F32)
    total = jnp.zeros((POS, 3 * C1), F32)
    for row, col in TAPS9:
        step = PAD + COLS * (row - 1) + col - 1
        window = padded[step : step + POS]
        if col != 1:
            window = jnp.where(column_mask(col - 1, (POS, D), 0), window, 0.0)
        tap = 3 * row + col
        weight = jnp.concatenate([weight_ref[tap + 9 * k] for k in range(3)], axis=1)
        total = total + jnp.dot(window.astype(BF16), weight, preferred_element_type=F32)
    to_next, to_last = total[:, 0:C1], total[:, 2 * C1 :]
    even = lax.axis_index("seq") % 2 == 0
    pair_ref[...] = jnp.where(even, to_next, to_last)
    keep_ref[...] = total[:, C1 : 2 * C1]
    cross_ref[...] = jnp.where(even, to_last, to_next)


def tap_weight(weight_ref, row, col):
    return jnp.concatenate([weight_ref[9 * k + 3 * row + col] for k in range(3)], axis=0)


def loss_cotangent(pair_ref, here_ref, cross_ref, weight_ref, bias_ref, packed_ref,
                   index_ref, blocks_ref, cots, padded, moved):
    even = lax.axis_index("seq") % 2 == 0
    zeros = jnp.zeros((PAD, 3 * C1), F32)
    padded[0:PAD] = zeros
    padded[PAD + POS :] = zeros
    pair, cross = pair_ref[...].astype(F32), cross_ref[...].astype(F32)
    frames = (jnp.where(even, cross, pair), here_ref[...].astype(F32), jnp.where(even, pair, cross))
    for k, value in enumerate(frames):
        padded[PAD : PAD + POS, k * C1 : (k + 1) * C1] = value
        narrow = value.astype(BF16)
        for block in range(16):
            blocks_ref[block, CHUNK + k * POS : CHUNK + (k + 1) * POS] = narrow
    for row, col in TAPS9:
        step = PAD + COLS * (row - 1) + col - 1
        window = padded[step : step + POS]
        if col != 1:
            window = jnp.where(column_mask(col - 1, (POS, 3 * C1), 0), window, 0.0)
        moved[3 * row + col] = window.astype(BF16)
    slabs = []
    for slab in range(16):
        part = packed_ref[slab, 0:CHUNK].astype(F32)
        slabs.append(
            jnp.concatenate([part[8 * n : 8 * n + 8] for n in range(4 * CO // 128)], axis=1)
        )
    pix = jnp.concatenate(slabs, axis=0)
    center = pix - jnp.mean(pix, axis=-1, keepdims=True)
    spread = jnp.mean(center * center, axis=-1, keepdims=True)
    normed = center * lax.rsqrt(spread + 1e-06)
    spot = lax.broadcasted_iota(jnp.int32, (POS, index_ref.shape[1]), 0)
    hits = jnp.sum((spot == index_ref[...]).astype(F32), axis=1, keepdims=True)
    scale = (2.0 / (4 * CO)) * hits
    predict = jnp.zeros((4 * POS, CO), F32)
    for row, col in TAPS9:
        lhs = jnp.concatenate(
            [moved[3 * (token_step(i, row) + 1) + token_step(j, col) + 1] for i, j in PHASES], axis=0
        )
        predict = predict + jnp.dot(
            lhs, tap_weight(weight_ref, row, col), preferred_element_type=F32
        )
    predict = predict + bias_ref[...]
    turned = []
    for k in range(4):
        cot = scale * (predict[k * POS : (k + 1) * POS] - normed[:, k * CO : (k + 1) * CO])
        cot = cot.astype(BF16)
        cots[k * POS : (k + 1) * POS] = cot
        turned.append(cot.astype(F32).T)
    width = CO // 16
    for block in range(16):
        blocks_ref[block, 0:CHUNK] = jnp.concatenate(
            [part[block * width : (block + 1) * width] for part in turned], axis=0
        ).astype(BF16)

def back_conv(cots, weight_ref, to_pair_ref, keep_ref, to_cross_ref, shifted):
    even = lax.axis_index("seq") % 2 == 0
    zeros = jnp.zeros((PAD, 3 * C1), F32)
    cot = cots[...]
    sums = {}
    for row, col in TAPS9:
        part = lax.dot_general(
            cot, tap_weight(weight_ref, row, col), (((1,), (1,)), ((), ())),
            preferred_element_type=F32,
        )
        for k, (i, j) in enumerate(PHASES):
            key = (token_step(i, row), token_step(j, col))
            piece = part[k * POS : (k + 1) * POS]
            sums[key] = sums[key] + piece if key in sums else piece
    total = sums[(0, 0)]
    for k, ((row, col), value) in enumerate(sums.items()):
        if (row, col) == (0, 0):
            continue
        if col != 0:
            value = jnp.where(column_mask(col, (POS, 3 * C1), 0), value, 0.0)
        shifted[k, 0:PAD] = zeros
        shifted[k, PAD + POS :] = zeros
        shifted[k, PAD : PAD + POS] = value
        step = PAD - COLS * row - col
        total = total + shifted[k, step : step + POS]
    to_last, to_next = total[:, 0:C1], total[:, 2 * C1 :]
    to_pair_ref[...] = jnp.where(even, to_next, to_last)
    keep_ref[...] = total[:, C1 : 2 * C1]
    to_cross_ref[...] = jnp.where(even, to_last, to_next)


def halved(pairs, level, keep_ref, send_ref):
    bit = lax.axis_index("dp") // STEPS[level] % 2
    for at, (zero, one) in enumerate(pairs):
        keep_ref[at] = jnp.where(bit == 0, zero, one)
        send_ref[at] = jnp.where(bit == 0, one, zero)


def hidden_values(pair_ref, keep_ref, cross_ref, bias_ref, zsum_ref, hidden_ref):
    zsum = pair_ref[...] + keep_ref[...] + cross_ref[...] + bias_ref[...]
    zsum_ref[...] = zsum
    hidden_ref[...] = jax.nn.gelu(zsum, approximate=True).astype(BF16)


def hidden_grads(pair_ref, keep_ref, cross_ref, zsum_ref, out_ref):
    grad = pair_ref[...] + keep_ref[...] + cross_ref[...]
    gelu_tanh = partial(jax.nn.gelu, approximate=True)
    out_ref[...] = jax.vjp(gelu_tanh, zsum_ref[...])[1](grad)[0].astype(BF16)


def second_grads(blocks_ref, before_ref, out_ref, left, right):
    del before_ref
    wide, thin = CO // 16, C1 // 16
    masks = {}
    for row in (-1, 0, 1):
        for col in (-1, 0, 1):
            masks[(row, col)] = spot_mask(row, col, (1, POS), 1)
    for clip in range(16):
        lanes = slice(clip * POS, (clip + 1) * POS)
        value = blocks_ref[clip, 0:CHUNK].astype(F32)
        parts = []
        for row, i in PAIRS:
            for col, j in PAIRS:
                phase = 2 * i + j
                part = value[phase * wide : (phase + 1) * wide]
                step = COLS * row + col
                if step != 0:
                    part = pltpu.roll(part, (POS - step) % POS, 1)
                    part = jnp.where(masks[(row, col)], part, 0.0)
                parts.append(part)
        left[:, lanes] = jnp.concatenate(parts, axis=0).astype(BF16)
        for k in range(3):
            right[lanes, k * C1 : (k + 1) * C1] = blocks_ref[
                clip, CHUNK + k * POS : CHUNK + (k + 1) * POS
            ]
    both = jnp.dot(left[...], right[...], preferred_element_type=F32)
    parts = []
    for k in range(3):
        for row in range(3):
            for col in range(3):
                value = None
                for row_pair in PAIRS_OF_TAP[row]:
                    for col_pair in PAIRS_OF_TAP[col]:
                        at = (4 * PAIRS.index(row_pair) + PAIRS.index(col_pair)) * wide
                        piece = both[at : at + wide, k * C1 : (k + 1) * C1]
                        value = piece if value is None else value + piece
                parts.append(value)
    parts.append(jnp.zeros((6 * 128 - 27 * wide, C1), F32))
    turned = jnp.concatenate(parts, axis=0).T
    for block in range(16):
        two = turned[block * thin : (block + 1) * thin]
        out_ref[block] = jnp.concatenate(
            [two[:, 128 * n : 128 * (n + 1)] for n in range(6)], axis=0
        ).astype(out_ref.dtype)


def half_sum(level, kept_ref, came_ref, keep_ref, send_ref):
    pairs = [
        tuple(kept_ref[at] + came_ref[at] for at in (two, two + 1))
        for two in range(0, kept_ref.shape[0], 2)
    ]
    halved(pairs, level, keep_ref, send_ref)


def last_sum(kept_ref, came_ref, out_ref):
    total = kept_ref[0] + came_ref[0]
    width = out_ref.shape[2]
    for k in range(27):
        out_ref[k] = total[:, k * width : (k + 1) * width]


def first_grads(packed_ref, gz_ref, keep_ref, send_ref, moved):
    width, thin = D // 16, C1 // 16
    zeros = jnp.zeros((9 * width, POS), BF16)
    moved[:, 0:POS] = zeros
    moved[:, 17 * POS :] = zeros
    for frame in range(16):
        value = packed_ref[frame, CHUNK:].astype(F32)
        parts = []
        for row, col in TAPS9:
            part = value
            step = COLS * (row - 1) + col - 1
            if step != 0:
                part = pltpu.roll(value, (POS - step) % POS, 1)
                part = jnp.where(spot_mask(row - 1, col - 1, (1, POS), 1), part, 0.0)
            parts.append(part)
        moved[:, (frame + 1) * POS : (frame + 2) * POS] = jnp.concatenate(parts, axis=0).astype(
            BF16
        )
    right = gz_ref[...].reshape(16 * POS, C1)
    parts = []
    for k in range(3):
        parts.append(
            jnp.dot(moved[:, k * POS : (k + 16) * POS], right, preferred_element_type=F32)
        )
    parts.append(jnp.zeros((7 * 128 - 27 * width, C1), F32))
    turned = jnp.concatenate(parts, axis=0).T
    order = [sum(step for n, step in enumerate(STEPS) if slot >> n & 1) for slot in range(16)]
    blocks = [turned[block * thin : (block + 1) * thin] for block in order]
    halved(zip(blocks[0::2], blocks[1::2]), 0, keep_ref, send_ref)


def summed(parts_ref, out_ref):
    total = parts_ref[0].astype(F32)
    for source in range(1, 16):
        total = total + parts_ref[source].astype(F32)
    _, rows, width = out_ref.shape
    total = jnp.concatenate(
        [total[rows * n : rows * (n + 1)] for n in range(total.shape[0] // rows)], axis=1
    )
    for k in range(27):
        out_ref[k] = total[:, k * width : (k + 1) * width]


def exchange(value, axis):
    return lax.all_to_all(value, axis, split_axis=0, concat_axis=0, tiled=True)


def swapped(value, step, axis="seq"):
    return lax.ppermute(value, axis, [(i, i ^ step) for i in range(16)])


def with_pair(value):
    return swapped(value, 1)


def with_cross(value):
    swaps = [(i, i + 1) for i in range(1, 15, 2)]
    return lax.ppermute(value, "seq", swaps + [(j, i) for i, j in swaps])


def per_device(tokens, conv_first, bias_first, conv_second, bias_second, pixels, mask_index):
    field = tokens.reshape(POS, D)
    packed = call(
        packed_inputs, struct((16, CHUNK + D // 16, POS), BF16), spots(VMEM, VMEM)
    )(pixels.reshape(16, 8, 4 * CO), field)
    plane = struct((POS, C1), F32)
    pair, keep, cross = call(
        first_conv,
        (plane, plane, plane),
        spots(VMEM, VMEM, pl.ANY),
        [pltpu.VMEM((POS + 2 * PAD, D), F32)],
    )(field, conv_first, packed)
    packed = exchange(packed, "seq")
    zsum, hidden = call(
        hidden_values,
        (plane, struct((POS, C1), BF16)),
        spots(*[VMEM] * 4),
        flops=FLOPS,
    )(with_pair(pair), keep, with_cross(cross), bias_first[None])

    blocks, cot = call(
        loss_cotangent,
        (struct((16, CHUNK + 3 * POS, POS), BF16), struct((4 * POS, CO), BF16)),
        spots(*[VMEM] * 7),
        [pltpu.VMEM((POS + 2 * PAD, 3 * C1), F32), pltpu.VMEM((9, POS, 3 * C1), BF16)],
    )(
        with_pair(hidden), hidden, with_cross(hidden), conv_second, bias_second[None],
        packed, mask_index,
    )
    pair, keep, cross = call(
        back_conv,
        (plane, plane, plane),
        spots(VMEM, VMEM),
        [pltpu.VMEM((9, POS + 2 * PAD, 3 * C1), F32)],
    )(cot, conv_second)
    blocks = exchange(blocks, "dp")
    grad_z = call(hidden_grads, struct((POS, C1), BF16), spots(*[VMEM] * 4))(
        with_pair(pair), keep, with_cross(cross), zsum
    )
    grad_z = lax.all_gather(grad_z, "seq")

    half = struct((8, C1 // 16, 7 * 128), F32)
    keep, send = call(
        first_grads,
        (half, half),
        spots(VMEM, VMEM),
        [pltpu.VMEM((9 * D // 16, 18 * POS), BF16)],
    )(packed, grad_z)
    grad_first_half = keep
    for level in (1, 2, 3):
        half = struct((8 >> level, C1 // 16, 7 * 128), F32)
        came = swapped(send, STEPS[level - 1], "dp")
        keep, send = call(
            partial(half_sum, level), (half, half), spots(VMEM, VMEM)
        )(keep, came)
    grad_first = call(last_sum, struct((27, C1 // 16, D // 16), F32), spots(VMEM, VMEM))(
        keep, swapped(send, STEPS[3], "dp")
    )
    second = call(
        second_grads,
        struct((16, 48, 128), BF16),
        spots(VMEM, pl.ANY),
        [pltpu.VMEM((CO, 16 * POS), BF16), pltpu.VMEM((16 * POS, CO), BF16)],
    )(blocks, grad_first_half)
    grad_second = call(summed, struct((27, C1 // 16, CO // 16), F32), spots(VMEM))(
        exchange(second, "seq")
    )
    return grad_first.transpose(0, 2, 1), grad_second


def solution(mesh):
    return jax.shard_map(
        per_device,
        mesh=mesh,
        in_specs=(
            P("dp", "seq", None, None, None),
            P(),
            P(),
            P(),
            P(),
            P("dp", None, "seq", None, None),
            P("dp", None),
        ),
        out_specs=(P(None, "seq", "dp"), P(None, "seq", "dp")),
        check_vma=False,
    )
```

```python
from functools import partial

import jax
import jax.numpy as jnp
from jax import lax
from jax.experimental import pallas as pl
from jax.experimental.pallas import tpu as pltpu
from jax.sharding import PartitionSpec as P

F32 = jnp.float32
BF16 = jnp.bfloat16
POS, COLS, PAD = 128, 4, 8
D, C1, CO = 512, 128, 384
CHUNK = 4 * CO // 16
FLOPS = 40_000_000_000
STEPS = (2, 1, 8, 4)
TAPS9 = [(row, col) for row in range(3) for col in range(3)]
PHASES = [(i, j) for i in range(2) for j in range(2)]
PAIRS = [(-1, 1), (0, 0), (0, 1), (1, 0)]
PAIRS_OF_TAP = [[(0, 1), (1, 0)], [(0, 0), (0, 1)], [(-1, 1), (0, 0)]]


def token_step(phase, tap):
    return (phase + tap - 1) // 2


def column_mask(step, shape, axis):
    column = lax.broadcasted_iota(jnp.int32, shape, axis) % COLS + step
    return (column >= 0) & (column < COLS)


def spot_mask(row_step, col_step, shape, axis):
    spot = lax.broadcasted_iota(jnp.int32, shape, axis)
    column = spot % COLS + col_step
    row = spot // COLS + row_step
    return (column >= 0) & (column < COLS) & (row >= 0) & (row < POS // COLS)


def call(body, out_shape, in_specs, scratch=(), flops=0, size=0, limit=16, **options):
    return pl.pallas_call(
        body,
        out_shape=out_shape,
        in_specs=in_specs,
        **options,
        scratch_shapes=list(scratch),
        compiler_params=pltpu.CompilerParams(vmem_limit_bytes=limit << 20),
        cost_estimate=pl.CostEstimate(flops=flops, bytes_accessed=size, transcendentals=0),
    )


def struct(shape, dtype):
    return jax.ShapeDtypeStruct(shape, dtype)


VMEM = pltpu.VMEM


def spots(*kinds):
    return [pl.BlockSpec(memory_space=kind) for kind in kinds]


def packed_inputs(pixel_ref, tokens_ref, out_ref):
    turned = tokens_ref[...].T
    width = D // 16
    for block in range(16):
        pix = pixel_ref[block].astype(F32)
        out_ref[block, 0:CHUNK] = jnp.concatenate(
            [pix[:, n * 128 : (n + 1) * 128] for n in range(4 * CO // 128)], axis=0
        ).astype(BF16)
        out_ref[block, CHUNK:] = turned[block * width : (block + 1) * width]


def first_conv(tokens_ref, weight_ref, before_ref, pair_ref, keep_ref, cross_ref, padded):
    del before_ref
    padded[0:PAD] = jnp.zeros((PAD, D), F32)
    padded[PAD + POS :] = jnp.zeros((PAD, D), F32)
    padded[PAD : PAD + POS] = tokens_ref[...].astype(F32)
    total = jnp.zeros((POS, 3 * C1), F32)
    for row, col in TAPS9:
        step = PAD + COLS * (row - 1) + col - 1
        window = padded[step : step + POS]
        if col != 1:
            window = jnp.where(column_mask(col - 1, (POS, D), 0), window, 0.0)
        tap = 3 * row + col
        weight = jnp.concatenate([weight_ref[tap + 9 * k] for k in range(3)], axis=1)
        total = total + jnp.dot(window.astype(BF16), weight, preferred_element_type=F32)
    to_next, to_last = total[:, 0:C1], total[:, 2 * C1 :]
    even = lax.axis_index("seq") % 2 == 0
    pair_ref[...] = jnp.where(even, to_next, to_last)
    keep_ref[...] = total[:, C1 : 2 * C1]
    cross_ref[...] = jnp.where(even, to_last, to_next)


def tap_weight(weight_ref, row, col):
    return jnp.concatenate([weight_ref[9 * k + 3 * row + col] for k in range(3)], axis=0)


def loss_cotangent(pair_ref, here_ref, cross_ref, weight_ref, bias_ref, packed_ref,
                   index_ref, blocks_ref, cots, padded, moved):
    even = lax.axis_index("seq") % 2 == 0
    zeros = jnp.zeros((PAD, 3 * C1), F32)
    padded[0:PAD] = zeros
    padded[PAD + POS :] = zeros
    pair, cross = pair_ref[...].astype(F32), cross_ref[...].astype(F32)
    frames = (jnp.where(even, cross, pair), here_ref[...].astype(F32), jnp.where(even, pair, cross))
    for k, value in enumerate(frames):
        padded[PAD : PAD + POS, k * C1 : (k + 1) * C1] = value
        narrow = value.astype(BF16)
        for block in range(16):
            blocks_ref[block, CHUNK + k * POS : CHUNK + (k + 1) * POS] = narrow
    for row, col in TAPS9:
        step = PAD + COLS * (row - 1) + col - 1
        window = padded[step : step + POS]
        if col != 1:
            window = jnp.where(column_mask(col - 1, (POS, 3 * C1), 0), window, 0.0)
        moved[3 * row + col] = window.astype(BF16)
    slabs = []
    for slab in range(16):
        part = packed_ref[slab, 0:CHUNK].astype(F32)
        slabs.append(
            jnp.concatenate([part[8 * n : 8 * n + 8] for n in range(4 * CO // 128)], axis=1)
        )
    pix = jnp.concatenate(slabs, axis=0)
    center = pix - jnp.mean(pix, axis=-1, keepdims=True)
    spread = jnp.mean(center * center, axis=-1, keepdims=True)
    normed = center * lax.rsqrt(spread + 1e-06)
    spot = lax.broadcasted_iota(jnp.int32, (POS, index_ref.shape[1]), 0)
    hits = jnp.sum((spot == index_ref[...]).astype(F32), axis=1, keepdims=True)
    scale = (2.0 / (4 * CO)) * hits
    predict = jnp.zeros((4 * POS, CO), F32)
    for row, col in TAPS9:
        lhs = jnp.concatenate(
            [moved[3 * (token_step(i, row) + 1) + token_step(j, col) + 1] for i, j in PHASES], axis=0
        )
        predict = predict + jnp.dot(
            lhs, tap_weight(weight_ref, row, col), preferred_element_type=F32
        )
    predict = predict + bias_ref[...]
    turned = []
    for k in range(4):
        cot = scale * (predict[k * POS : (k + 1) * POS] - normed[:, k * CO : (k + 1) * CO])
        cot = cot.astype(BF16)
        cots[k * POS : (k + 1) * POS] = cot
        turned.append(cot.astype(F32).T)
    width = CO // 16
    for block in range(16):
        blocks_ref[block, 0:CHUNK] = jnp.concatenate(
            [part[block * width : (block + 1) * width] for part in turned], axis=0
        ).astype(BF16)

def back_conv(cots, weight_ref, to_pair_ref, keep_ref, to_cross_ref, shifted):
    even = lax.axis_index("seq") % 2 == 0
    zeros = jnp.zeros((PAD, 3 * C1), F32)
    cot = cots[...]
    sums = {}
    for row, col in TAPS9:
        part = lax.dot_general(
            cot, tap_weight(weight_ref, row, col), (((1,), (1,)), ((), ())),
            preferred_element_type=F32,
        )
        for k, (i, j) in enumerate(PHASES):
            key = (token_step(i, row), token_step(j, col))
            piece = part[k * POS : (k + 1) * POS]
            sums[key] = sums[key] + piece if key in sums else piece
    total = sums[(0, 0)]
    for k, ((row, col), value) in enumerate(sums.items()):
        if (row, col) == (0, 0):
            continue
        if col != 0:
            value = jnp.where(column_mask(col, (POS, 3 * C1), 0), value, 0.0)
        shifted[k, 0:PAD] = zeros
        shifted[k, PAD + POS :] = zeros
        shifted[k, PAD : PAD + POS] = value
        step = PAD - COLS * row - col
        total = total + shifted[k, step : step + POS]
    to_last, to_next = total[:, 0:C1], total[:, 2 * C1 :]
    to_pair_ref[...] = jnp.where(even, to_next, to_last)
    keep_ref[...] = total[:, C1 : 2 * C1]
    to_cross_ref[...] = jnp.where(even, to_last, to_next)


def halved(pairs, level, keep_ref, send_ref):
    bit = lax.axis_index("dp") // STEPS[level] % 2
    for at, (zero, one) in enumerate(pairs):
        keep_ref[at] = jnp.where(bit == 0, zero, one)
        send_ref[at] = jnp.where(bit == 0, one, zero)


def hidden_values(pair_ref, keep_ref, cross_ref, bias_ref, zsum_ref, hidden_ref):
    zsum = pair_ref[...] + keep_ref[...] + cross_ref[...] + bias_ref[...]
    zsum_ref[...] = zsum
    hidden_ref[...] = jax.nn.gelu(zsum, approximate=True).astype(BF16)


def hidden_grads(pair_ref, keep_ref, cross_ref, zsum_ref, out_ref):
    grad = pair_ref[...] + keep_ref[...] + cross_ref[...]
    gelu_tanh = partial(jax.nn.gelu, approximate=True)
    out_ref[...] = jax.vjp(gelu_tanh, zsum_ref[...])[1](grad)[0].astype(BF16)


def second_grads(blocks_ref, before_ref, out_ref, left, right):
    del before_ref
    wide, thin = CO // 16, C1 // 16
    masks = {}
    for row in (-1, 0, 1):
        for col in (-1, 0, 1):
            masks[(row, col)] = spot_mask(row, col, (1, POS), 1)
    for clip in range(16):
        lanes = slice(clip * POS, (clip + 1) * POS)
        value = blocks_ref[clip, 0:CHUNK].astype(F32)
        parts = []
        for row, i in PAIRS:
            for col, j in PAIRS:
                phase = 2 * i + j
                part = value[phase * wide : (phase + 1) * wide]
                step = COLS * row + col
                if step != 0:
                    part = pltpu.roll(part, (POS - step) % POS, 1)
                    part = jnp.where(masks[(row, col)], part, 0.0)
                parts.append(part)
        left[:, lanes] = jnp.concatenate(parts, axis=0).astype(BF16)
        for k in range(3):
            right[lanes, k * C1 : (k + 1) * C1] = blocks_ref[
                clip, CHUNK + k * POS : CHUNK + (k + 1) * POS
            ]
    both = jnp.dot(left[...], right[...], preferred_element_type=F32)
    parts = []
    for k in range(3):
        for row in range(3):
            for col in range(3):
                value = None
                for row_pair in PAIRS_OF_TAP[row]:
                    for col_pair in PAIRS_OF_TAP[col]:
                        at = (4 * PAIRS.index(row_pair) + PAIRS.index(col_pair)) * wide
                        piece = both[at : at + wide, k * C1 : (k + 1) * C1]
                        value = piece if value is None else value + piece
                parts.append(value)
    parts.append(jnp.zeros((6 * 128 - 27 * wide, C1), F32))
    turned = jnp.concatenate(parts, axis=0).T
    for block in range(16):
        two = turned[block * thin : (block + 1) * thin]
        out_ref[block] = jnp.concatenate(
            [two[:, 128 * n : 128 * (n + 1)] for n in range(6)], axis=0
        ).astype(out_ref.dtype)


def half_sum(level, kept_ref, came_ref, keep_ref, send_ref):
    pairs = [
        tuple(kept_ref[at] + came_ref[at] for at in (two, two + 1))
        for two in range(0, kept_ref.shape[0], 2)
    ]
    halved(pairs, level, keep_ref, send_ref)


def last_sum(kept_ref, came_ref, before_ref, out_ref):
    del before_ref
    total = kept_ref[0] + came_ref[0]
    width = out_ref.shape[2]
    for k in range(27):
        out_ref[k] = total[:, k * width : (k + 1) * width]


def first_grads(packed_ref, gz_ref, keep_ref, send_ref, moved):
    width, thin = D // 16, C1 // 16
    zeros = jnp.zeros((9 * width, POS), BF16)
    moved[:, 0:POS] = zeros
    moved[:, 17 * POS :] = zeros
    for frame in range(16):
        value = packed_ref[frame, CHUNK:].astype(F32)
        parts = []
        for row, col in TAPS9:
            part = value
            step = COLS * (row - 1) + col - 1
            if step != 0:
                part = pltpu.roll(value, (POS - step) % POS, 1)
                part = jnp.where(spot_mask(row - 1, col - 1, (1, POS), 1), part, 0.0)
            parts.append(part)
        moved[:, (frame + 1) * POS : (frame + 2) * POS] = jnp.concatenate(parts, axis=0).astype(
            BF16
        )
    right = gz_ref[...].reshape(16 * POS, C1)
    parts = []
    for k in range(3):
        parts.append(
            jnp.dot(moved[:, k * POS : (k + 16) * POS], right, preferred_element_type=F32)
        )
    parts.append(jnp.zeros((7 * 128 - 27 * width, C1), F32))
    turned = jnp.concatenate(parts, axis=0).T
    order = [sum(step for n, step in enumerate(STEPS) if slot >> n & 1) for slot in range(16)]
    blocks = [turned[block * thin : (block + 1) * thin] for block in order]
    halved(zip(blocks[0::2], blocks[1::2]), 0, keep_ref, send_ref)


def summed(parts_ref, out_ref):
    total = parts_ref[0].astype(F32)
    for source in range(1, 16):
        total = total + parts_ref[source].astype(F32)
    _, rows, width = out_ref.shape
    total = jnp.concatenate(
        [total[rows * n : rows * (n + 1)] for n in range(total.shape[0] // rows)], axis=1
    )
    for k in range(27):
        out_ref[k] = total[:, k * width : (k + 1) * width]


def exchange(value, axis):
    return lax.all_to_all(value, axis, split_axis=0, concat_axis=0, tiled=True)


def swapped(value, step, axis="seq"):
    return lax.ppermute(value, axis, [(i, i ^ step) for i in range(16)])


def with_pair(value):
    return swapped(value, 1)


def with_cross(value):
    swaps = [(i, i + 1) for i in range(1, 15, 2)]
    return lax.ppermute(value, "seq", swaps + [(j, i) for i, j in swaps])


def per_device(tokens, conv_first, bias_first, conv_second, bias_second, pixels, mask_index):
    field = tokens.reshape(POS, D)
    packed = call(
        packed_inputs, struct((16, CHUNK + D // 16, POS), BF16), spots(VMEM, VMEM), flops=FLOPS // 10
    )(pixels.reshape(16, 8, 4 * CO), field)
    plane = struct((POS, C1), F32)
    pair, keep, cross = call(
        first_conv,
        (plane, plane, plane),
        spots(VMEM, VMEM, pl.ANY),
        [pltpu.VMEM((POS + 2 * PAD, D), F32)],
    )(field, conv_first, packed)
    packed = exchange(packed, "seq")
    zsum, hidden = call(
        hidden_values,
        (plane, struct((POS, C1), BF16)),
        spots(*[VMEM] * 4),
        flops=FLOPS,
    )(with_pair(pair), keep, with_cross(cross), bias_first[None])

    blocks, cot = call(
        loss_cotangent,
        (struct((16, CHUNK + 3 * POS, POS), BF16), struct((4 * POS, CO), BF16)),
        spots(*[VMEM] * 7),
        [pltpu.VMEM((POS + 2 * PAD, 3 * C1), F32), pltpu.VMEM((9, POS, 3 * C1), BF16)],
    )(
        with_pair(hidden), hidden, with_cross(hidden), conv_second, bias_second[None],
        packed, mask_index,
    )
    pair, keep, cross = call(
        back_conv,
        (plane, plane, plane),
        spots(VMEM, VMEM),
        [pltpu.VMEM((9, POS + 2 * PAD, 3 * C1), F32)],
        size=4 << 20,
    )(cot, conv_second)
    blocks = exchange(blocks, "dp")
    grad_z = call(hidden_grads, struct((POS, C1), BF16), spots(*[VMEM] * 4))(
        with_pair(pair), keep, with_cross(cross), zsum
    )
    grad_z = lax.all_gather(grad_z, "seq")

    half = struct((8, C1 // 16, 7 * 128), F32)
    keep, send = call(
        first_grads,
        (half, half),
        spots(VMEM, VMEM),
        [pltpu.VMEM((9 * D // 16, 18 * POS), BF16)],
    )(packed, grad_z)
    grad_first_half = keep
    for level in (1, 2, 3):
        half = struct((8 >> level, C1 // 16, 7 * 128), F32)
        came = swapped(send, STEPS[level - 1], "dp")
        keep, send = call(
            partial(half_sum, level), (half, half), spots(VMEM, VMEM)
        )(keep, came)
    second = call(
        second_grads,
        struct((16, 48, 128), BF16),
        spots(VMEM, pl.ANY),
        [pltpu.VMEM((CO, 16 * POS), BF16), pltpu.VMEM((16 * POS, CO), BF16)],
        size=4 << 20,
    )(blocks, grad_first_half)
    grad_second = call(summed, struct((27, C1 // 16, CO // 16), F32), spots(VMEM))(
        exchange(second, "seq")
    )
    grad_second = grad_second.transpose(1, 2, 0)
    grad_first = call(last_sum, struct((27, C1 // 16, D // 16), F32), spots(VMEM, VMEM, pl.ANY))(
        keep, swapped(send, STEPS[3], "dp"), grad_second
    )
    return grad_first.transpose(0, 2, 1), grad_second.transpose(2, 0, 1)


def solution(mesh):
    return jax.shard_map(
        per_device,
        mesh=mesh,
        in_specs=(
            P("dp", "seq", None, None, None),
            P(),
            P(),
            P(),
            P(),
            P("dp", None, "seq", None, None),
            P("dp", None),
        ),
        out_specs=(P(None, "seq", "dp"), P(None, "seq", "dp")),
        check_vma=False,
    )
```

```python
from functools import partial

import jax
import jax.numpy as jnp
from jax import lax
from jax.experimental import pallas as pl
from jax.experimental.pallas import tpu as pltpu
from jax.sharding import PartitionSpec as P

F32 = jnp.float32
BF16 = jnp.bfloat16
POS, COLS, PAD = 128, 4, 8
D, C1, CO = 512, 128, 384
CHUNK = 4 * CO // 16
FLOPS = 40_000_000_000
STEPS = (2, 1, 8, 4)
TAPS9 = [(row, col) for row in range(3) for col in range(3)]
PHASES = [(i, j) for i in range(2) for j in range(2)]
PAIRS = [(-1, 1), (0, 0), (0, 1), (1, 0)]
PAIRS_OF_TAP = [[(0, 1), (1, 0)], [(0, 0), (0, 1)], [(-1, 1), (0, 0)]]


def token_step(phase, tap):
    return (phase + tap - 1) // 2


def column_mask(step, shape, axis):
    column = lax.broadcasted_iota(jnp.int32, shape, axis) % COLS + step
    return (column >= 0) & (column < COLS)


def spot_mask(row_step, col_step, shape, axis):
    spot = lax.broadcasted_iota(jnp.int32, shape, axis)
    column = spot % COLS + col_step
    row = spot // COLS + row_step
    return (column >= 0) & (column < COLS) & (row >= 0) & (row < POS // COLS)


def call(body, out_shape, in_specs, scratch=(), flops=0, size=0, limit=16, **options):
    return pl.pallas_call(
        body,
        out_shape=out_shape,
        in_specs=in_specs,
        **options,
        scratch_shapes=list(scratch),
        compiler_params=pltpu.CompilerParams(vmem_limit_bytes=limit << 20),
        cost_estimate=pl.CostEstimate(flops=flops, bytes_accessed=size, transcendentals=0),
    )


def struct(shape, dtype):
    return jax.ShapeDtypeStruct(shape, dtype)


VMEM = pltpu.VMEM


def spots(*kinds):
    return [pl.BlockSpec(memory_space=kind) for kind in kinds]


def packed_inputs(pixel_ref, tokens_ref, out_ref, field_ref):
    tokens = tokens_ref[...].astype(F32).reshape(POS, D).astype(BF16)
    field_ref[...] = tokens
    turned = tokens.T
    width = D // 16
    for block in range(16):
        pix = pixel_ref[block].astype(F32).reshape(8, 4 * CO)
        out_ref[block, 0:CHUNK] = jnp.concatenate(
            [pix[:, n * 128 : (n + 1) * 128] for n in range(4 * CO // 128)], axis=0
        ).astype(BF16)
        out_ref[block, CHUNK:] = turned[block * width : (block + 1) * width]


def first_conv(tokens_ref, weight_ref, before_ref, pair_ref, keep_ref, cross_ref, padded):
    del before_ref
    padded[0:PAD] = jnp.zeros((PAD, D), F32)
    padded[PAD + POS :] = jnp.zeros((PAD, D), F32)
    padded[PAD : PAD + POS] = tokens_ref[...].astype(F32)
    total = jnp.zeros((POS, 3 * C1), F32)
    for row, col in TAPS9:
        step = PAD + COLS * (row - 1) + col - 1
        window = padded[step : step + POS]
        if col != 1:
            window = jnp.where(column_mask(col - 1, (POS, D), 0), window, 0.0)
        tap = 3 * row + col
        weight = jnp.concatenate([weight_ref[tap + 9 * k] for k in range(3)], axis=1)
        total = total + jnp.dot(window.astype(BF16), weight, preferred_element_type=F32)
    to_next, to_last = total[:, 0:C1], total[:, 2 * C1 :]
    even = lax.axis_index("seq") % 2 == 0
    pair_ref[...] = jnp.where(even, to_next, to_last)
    keep_ref[...] = total[:, C1 : 2 * C1]
    cross_ref[...] = jnp.where(even, to_last, to_next)


def tap_weight(weight_ref, row, col):
    return jnp.concatenate([weight_ref[9 * k + 3 * row + col] for k in range(3)], axis=0)


def loss_cotangent(pair_ref, here_ref, cross_ref, weight_ref, bias_ref, packed_ref,
                   index_ref, blocks_ref, cots, padded, moved):
    even = lax.axis_index("seq") % 2 == 0
    zeros = jnp.zeros((PAD, 3 * C1), F32)
    padded[0:PAD] = zeros
    padded[PAD + POS :] = zeros
    pair, cross = pair_ref[...].astype(F32), cross_ref[...].astype(F32)
    frames = (jnp.where(even, cross, pair), here_ref[...].astype(F32), jnp.where(even, pair, cross))
    for k, value in enumerate(frames):
        padded[PAD : PAD + POS, k * C1 : (k + 1) * C1] = value
        narrow = value.astype(BF16)
        for block in range(16):
            blocks_ref[block, CHUNK + k * POS : CHUNK + (k + 1) * POS] = narrow
    for row, col in TAPS9:
        step = PAD + COLS * (row - 1) + col - 1
        window = padded[step : step + POS]
        if col != 1:
            window = jnp.where(column_mask(col - 1, (POS, 3 * C1), 0), window, 0.0)
        moved[3 * row + col] = window.astype(BF16)
    slabs = []
    for slab in range(16):
        part = packed_ref[slab, 0:CHUNK].astype(F32)
        slabs.append(
            jnp.concatenate([part[8 * n : 8 * n + 8] for n in range(4 * CO // 128)], axis=1)
        )
    pix = jnp.concatenate(slabs, axis=0)
    center = pix - jnp.mean(pix, axis=-1, keepdims=True)
    spread = jnp.mean(center * center, axis=-1, keepdims=True)
    normed = center * lax.rsqrt(spread + 1e-06)
    spot = lax.broadcasted_iota(jnp.int32, (POS, index_ref.shape[1]), 0)
    hits = jnp.sum((spot == index_ref[...]).astype(F32), axis=1, keepdims=True)
    scale = (2.0 / (4 * CO)) * hits
    predict = jnp.zeros((4 * POS, CO), F32)
    for row, col in TAPS9:
        lhs = jnp.concatenate(
            [moved[3 * (token_step(i, row) + 1) + token_step(j, col) + 1] for i, j in PHASES], axis=0
        )
        predict = predict + jnp.dot(
            lhs, tap_weight(weight_ref, row, col), preferred_element_type=F32
        )
    predict = predict + bias_ref[...]
    turned = []
    for k in range(4):
        cot = scale * (predict[k * POS : (k + 1) * POS] - normed[:, k * CO : (k + 1) * CO])
        cot = cot.astype(BF16)
        cots[k * POS : (k + 1) * POS] = cot
        turned.append(cot.astype(F32).T)
    width = CO // 16
    for block in range(16):
        blocks_ref[block, 0:CHUNK] = jnp.concatenate(
            [part[block * width : (block + 1) * width] for part in turned], axis=0
        ).astype(BF16)

def back_conv(cots, weight_ref, to_pair_ref, keep_ref, to_cross_ref, shifted):
    even = lax.axis_index("seq") % 2 == 0
    zeros = jnp.zeros((PAD, 3 * C1), F32)
    cot = cots[...]
    sums = {}
    for row, col in TAPS9:
        part = lax.dot_general(
            cot, tap_weight(weight_ref, row, col), (((1,), (1,)), ((), ())),
            preferred_element_type=F32,
        )
        for k, (i, j) in enumerate(PHASES):
            key = (token_step(i, row), token_step(j, col))
            piece = part[k * POS : (k + 1) * POS]
            sums[key] = sums[key] + piece if key in sums else piece
    total = sums[(0, 0)]
    for k, ((row, col), value) in enumerate(sums.items()):
        if (row, col) == (0, 0):
            continue
        if col != 0:
            value = jnp.where(column_mask(col, (POS, 3 * C1), 0), value, 0.0)
        shifted[k, 0:PAD] = zeros
        shifted[k, PAD + POS :] = zeros
        shifted[k, PAD : PAD + POS] = value
        step = PAD - COLS * row - col
        total = total + shifted[k, step : step + POS]
    to_last, to_next = total[:, 0:C1], total[:, 2 * C1 :]
    to_pair_ref[...] = jnp.where(even, to_next, to_last)
    keep_ref[...] = total[:, C1 : 2 * C1]
    to_cross_ref[...] = jnp.where(even, to_last, to_next)


def halved(pairs, level, keep_ref, send_ref):
    bit = lax.axis_index("dp") // STEPS[level] % 2
    for at, (zero, one) in enumerate(pairs):
        keep_ref[at] = jnp.where(bit == 0, zero, one)
        send_ref[at] = jnp.where(bit == 0, one, zero)


def hidden_values(pair_ref, keep_ref, cross_ref, bias_ref, zsum_ref, hidden_ref):
    zsum = pair_ref[...] + keep_ref[...] + cross_ref[...] + bias_ref[...]
    zsum_ref[...] = zsum
    hidden_ref[...] = jax.nn.gelu(zsum, approximate=True).astype(BF16)


def hidden_grads(pair_ref, keep_ref, cross_ref, zsum_ref, out_ref):
    grad = pair_ref[...] + keep_ref[...] + cross_ref[...]
    gelu_tanh = partial(jax.nn.gelu, approximate=True)
    out_ref[...] = jax.vjp(gelu_tanh, zsum_ref[...])[1](grad)[0].astype(BF16)


def second_grads(source_ref, before_ref, out_ref, left, right, blocks_ref, sems):
    del before_ref
    copies = [
        pltpu.make_async_copy(
            source_ref.at[4 * n : 4 * n + 4], blocks_ref.at[4 * n : 4 * n + 4], sems.at[n]
        )
        for n in range(4)
    ]
    for copy in copies:
        copy.start()
    wide, thin = CO // 16, C1 // 16
    masks = {}
    for row in (-1, 0, 1):
        for col in (-1, 0, 1):
            masks[(row, col)] = spot_mask(row, col, (1, POS), 1)
    for clip in range(16):
        lanes = slice(clip * POS, (clip + 1) * POS)
        if clip % 4 == 0:
            copies[clip // 4].wait()
        value = blocks_ref[clip, 0:CHUNK].astype(F32)
        parts = []
        for row, i in PAIRS:
            for col, j in PAIRS:
                phase = 2 * i + j
                part = value[phase * wide : (phase + 1) * wide]
                step = COLS * row + col
                if step != 0:
                    part = pltpu.roll(part, (POS - step) % POS, 1)
                    part = jnp.where(masks[(row, col)], part, 0.0)
                parts.append(part)
        left[:, lanes] = jnp.concatenate(parts, axis=0).astype(BF16)
        for k in range(3):
            right[lanes, k * C1 : (k + 1) * C1] = blocks_ref[
                clip, CHUNK + k * POS : CHUNK + (k + 1) * POS
            ]
    both = jnp.dot(left[...], right[...], preferred_element_type=F32)
    parts = []
    for k in range(3):
        for row in range(3):
            for col in range(3):
                value = None
                for row_pair in PAIRS_OF_TAP[row]:
                    for col_pair in PAIRS_OF_TAP[col]:
                        at = (4 * PAIRS.index(row_pair) + PAIRS.index(col_pair)) * wide
                        piece = both[at : at + wide, k * C1 : (k + 1) * C1]
                        value = piece if value is None else value + piece
                parts.append(value)
    parts.append(jnp.zeros((6 * 128 - 27 * wide, C1), F32))
    turned = jnp.concatenate(parts, axis=0).T
    for block in range(16):
        two = turned[block * thin : (block + 1) * thin]
        out_ref[block] = jnp.concatenate(
            [two[:, 128 * n : 128 * (n + 1)] for n in range(6)], axis=0
        ).astype(out_ref.dtype)


def half_sum(level, kept_ref, came_ref, keep_ref, send_ref):
    pairs = [
        tuple(kept_ref[at] + came_ref[at] for at in (two, two + 1))
        for two in range(0, kept_ref.shape[0], 2)
    ]
    halved(pairs, level, keep_ref, send_ref)


def last_sum(kept_ref, came_ref, before_ref, out_ref):
    del before_ref
    total = kept_ref[0] + came_ref[0]
    width = out_ref.shape[2]
    for k in range(27):
        out_ref[k] = total[:, k * width : (k + 1) * width]


def first_grads(packed_ref, gz_ref, keep_ref, send_ref, moved):
    width, thin = D // 16, C1 // 16
    zeros = jnp.zeros((9 * width, POS), BF16)
    moved[:, 0:POS] = zeros
    moved[:, 17 * POS :] = zeros
    for frame in range(16):
        value = packed_ref[frame, CHUNK:].astype(F32)
        parts = []
        for row, col in TAPS9:
            part = value
            step = COLS * (row - 1) + col - 1
            if step != 0:
                part = pltpu.roll(value, (POS - step) % POS, 1)
                part = jnp.where(spot_mask(row - 1, col - 1, (1, POS), 1), part, 0.0)
            parts.append(part)
        moved[:, (frame + 1) * POS : (frame + 2) * POS] = jnp.concatenate(parts, axis=0).astype(
            BF16
        )
    right = gz_ref[...].reshape(16 * POS, C1)
    parts = []
    for k in range(3):
        parts.append(
            jnp.dot(moved[:, k * POS : (k + 16) * POS], right, preferred_element_type=F32)
        )
    parts.append(jnp.zeros((7 * 128 - 27 * width, C1), F32))
    turned = jnp.concatenate(parts, axis=0).T
    order = [sum(step for n, step in enumerate(STEPS) if slot >> n & 1) for slot in range(16)]
    blocks = [turned[block * thin : (block + 1) * thin] for block in order]
    halved(zip(blocks[0::2], blocks[1::2]), 0, keep_ref, send_ref)


def summed(parts_ref, out_ref):
    total = parts_ref[0].astype(F32)
    for source in range(1, 16):
        total = total + parts_ref[source].astype(F32)
    _, rows, width = out_ref.shape
    total = jnp.concatenate(
        [total[rows * n : rows * (n + 1)] for n in range(total.shape[0] // rows)], axis=1
    )
    for k in range(27):
        out_ref[k] = total[:, k * width : (k + 1) * width]


def exchange(value, axis):
    return lax.all_to_all(value, axis, split_axis=0, concat_axis=0, tiled=True)


def swapped(value, step, axis="seq"):
    return lax.ppermute(value, axis, [(i, i ^ step) for i in range(16)])


def with_pair(value):
    return swapped(value, 1)


def with_cross(value):
    swaps = [(i, i + 1) for i in range(1, 15, 2)]
    return lax.ppermute(value, "seq", swaps + [(j, i) for i, j in swaps])


def per_device(tokens, conv_first, bias_first, conv_second, bias_second, pixels, mask_index):
    packed, field = call(
        packed_inputs,
        (struct((16, CHUNK + D // 16, POS), BF16), struct((POS, D), BF16)),
        spots(VMEM, VMEM),
        flops=FLOPS // 10,
    )(pixels[0], tokens[0, 0])
    plane = struct((POS, C1), F32)
    pair, keep, cross = call(
        first_conv,
        (plane, plane, plane),
        spots(VMEM, VMEM, pl.ANY),
        [pltpu.VMEM((POS + 2 * PAD, D), F32)],
    )(field, conv_first, packed)
    packed = exchange(packed, "seq")
    zsum, hidden = call(
        hidden_values,
        (plane, struct((POS, C1), BF16)),
        spots(*[VMEM] * 4),
        flops=FLOPS,
    )(with_pair(pair), keep, with_cross(cross), bias_first[None])

    blocks, cot = call(
        loss_cotangent,
        (struct((16, CHUNK + 3 * POS, POS), BF16), struct((4 * POS, CO), BF16)),
        spots(*[VMEM] * 7),
        [pltpu.VMEM((POS + 2 * PAD, 3 * C1), F32), pltpu.VMEM((9, POS, 3 * C1), BF16)],
    )(
        with_pair(hidden), hidden, with_cross(hidden), conv_second, bias_second[None],
        packed, mask_index,
    )
    pair, keep, cross = call(
        back_conv,
        (plane, plane, plane),
        spots(VMEM, VMEM),
        [pltpu.VMEM((9, POS + 2 * PAD, 3 * C1), F32)],
        size=4 << 20,
    )(cot, conv_second)
    blocks = exchange(blocks, "dp")
    grad_z = call(hidden_grads, struct((POS, C1), BF16), spots(*[VMEM] * 4))(
        with_pair(pair), keep, with_cross(cross), zsum
    )
    grad_z = lax.all_gather(grad_z, "seq")

    half = struct((8, C1 // 16, 7 * 128), F32)
    keep, send = call(
        first_grads,
        (half, half),
        spots(VMEM, VMEM),
        [pltpu.VMEM((9 * D // 16, 18 * POS), BF16)],
    )(packed, grad_z)
    grad_first_half = keep
    for level in (1, 2, 3):
        half = struct((8 >> level, C1 // 16, 7 * 128), F32)
        came = swapped(send, STEPS[level - 1], "dp")
        keep, send = call(
            partial(half_sum, level), (half, half), spots(VMEM, VMEM)
        )(keep, came)
    second = call(
        second_grads,
        struct((16, 48, 128), BF16),
        spots(pl.ANY, pl.ANY),
        [
            pltpu.VMEM((CO, 16 * POS), BF16),
            pltpu.VMEM((16 * POS, CO), BF16),
            pltpu.VMEM((16, CHUNK + 3 * POS, POS), BF16),
            pltpu.SemaphoreType.DMA((4,)),
        ],
        size=4 << 20,
    )(blocks, grad_first_half)
    grad_second = call(summed, struct((27, C1 // 16, CO // 16), F32), spots(VMEM))(
        exchange(second, "seq")
    )
    grad_second = grad_second.transpose(1, 2, 0)
    grad_first = call(last_sum, struct((27, C1 // 16, D // 16), F32), spots(VMEM, VMEM, pl.ANY))(
        keep, swapped(send, STEPS[3], "dp"), grad_second
    )
    return grad_first.transpose(0, 2, 1), grad_second.transpose(2, 0, 1)


def solution(mesh):
    return jax.shard_map(
        per_device,
        mesh=mesh,
        in_specs=(
            P("dp", "seq", None, None, None),
            P(),
            P(),
            P(),
            P(),
            P("dp", None, "seq", None, None),
            P("dp", None),
        ),
        out_specs=(P(None, "seq", "dp"), P(None, "seq", "dp")),
        check_vma=False,
    )
```

```python
from functools import partial

import jax
import jax.numpy as jnp
from jax import lax
from jax.experimental import pallas as pl
from jax.experimental.pallas import tpu as pltpu
from jax.sharding import PartitionSpec as P

F32 = jnp.float32
BF16 = jnp.bfloat16
POS, COLS, PAD = 128, 4, 8
D, C1, CO = 512, 128, 384
CHUNK = 4 * CO // 16
FLOPS = 40_000_000_000
STEPS = (2, 1, 8, 4)
TAPS9 = [(row, col) for row in range(3) for col in range(3)]
PHASES = [(i, j) for i in range(2) for j in range(2)]
PAIRS = [(-1, 1), (0, 0), (0, 1), (1, 0)]
PAIRS_OF_TAP = [[(0, 1), (1, 0)], [(0, 0), (0, 1)], [(-1, 1), (0, 0)]]


def token_step(phase, tap):
    return (phase + tap - 1) // 2


def column_mask(step, shape, axis):
    column = lax.broadcasted_iota(jnp.int32, shape, axis) % COLS + step
    return (column >= 0) & (column < COLS)


def spot_mask(row_step, col_step, shape, axis):
    spot = lax.broadcasted_iota(jnp.int32, shape, axis)
    column = spot % COLS + col_step
    row = spot // COLS + row_step
    return (column >= 0) & (column < COLS) & (row >= 0) & (row < POS // COLS)


def call(body, out_shape, in_specs, scratch=(), flops=0, size=0, limit=16, **options):
    return pl.pallas_call(
        body,
        out_shape=out_shape,
        in_specs=in_specs,
        **options,
        scratch_shapes=list(scratch),
        compiler_params=pltpu.CompilerParams(vmem_limit_bytes=limit << 20),
        cost_estimate=pl.CostEstimate(flops=flops, bytes_accessed=size, transcendentals=0),
    )


def struct(shape, dtype):
    return jax.ShapeDtypeStruct(shape, dtype)


VMEM = pltpu.VMEM


def spots(*kinds):
    return [pl.BlockSpec(memory_space=kind) for kind in kinds]


def packed_inputs(pixel_source, tokens_source, out_ref, field_ref, pixel_ref, tokens_ref, sems):
    copies = [
        pltpu.make_async_copy(source, target, sems.at[n])
        for n, (source, target) in enumerate(
            ((tokens_source, tokens_ref), (pixel_source, pixel_ref))
        )
    ]
    for copy in copies:
        copy.start()
    copies[0].wait()
    tokens = tokens_ref[...].astype(F32).reshape(POS, D).astype(BF16)
    field_ref[...] = tokens
    turned = tokens.T
    width = D // 16
    copies[1].wait()
    for block in range(16):
        pix = pixel_ref[block].astype(F32).reshape(8, 4 * CO)
        out_ref[block, 0:CHUNK] = jnp.concatenate(
            [pix[:, n * 128 : (n + 1) * 128] for n in range(4 * CO // 128)], axis=0
        ).astype(BF16)
        out_ref[block, CHUNK:] = turned[block * width : (block + 1) * width]


def first_conv(tokens_ref, weight_ref, before_ref, pair_ref, keep_ref, cross_ref, padded):
    del before_ref
    padded[0:PAD] = jnp.zeros((PAD, D), F32)
    padded[PAD + POS :] = jnp.zeros((PAD, D), F32)
    padded[PAD : PAD + POS] = tokens_ref[...].astype(F32)
    total = jnp.zeros((POS, 3 * C1), F32)
    for row, col in TAPS9:
        step = PAD + COLS * (row - 1) + col - 1
        window = padded[step : step + POS]
        if col != 1:
            window = jnp.where(column_mask(col - 1, (POS, D), 0), window, 0.0)
        tap = 3 * row + col
        weight = jnp.concatenate([weight_ref[tap + 9 * k] for k in range(3)], axis=1)
        total = total + jnp.dot(window.astype(BF16), weight, preferred_element_type=F32)
    to_next, to_last = total[:, 0:C1], total[:, 2 * C1 :]
    even = lax.axis_index("seq") % 2 == 0
    pair_ref[...] = jnp.where(even, to_next, to_last)
    keep_ref[...] = total[:, C1 : 2 * C1]
    cross_ref[...] = jnp.where(even, to_last, to_next)


def tap_weight(weight_ref, row, col):
    return jnp.concatenate([weight_ref[9 * k + 3 * row + col] for k in range(3)], axis=0)


def loss_cotangent(pair_ref, here_ref, cross_ref, weight_ref, bias_ref, packed_ref,
                   index_ref, blocks_ref, cots, padded, moved):
    even = lax.axis_index("seq") % 2 == 0
    zeros = jnp.zeros((PAD, 3 * C1), F32)
    padded[0:PAD] = zeros
    padded[PAD + POS :] = zeros
    pair, cross = pair_ref[...].astype(F32), cross_ref[...].astype(F32)
    frames = (jnp.where(even, cross, pair), here_ref[...].astype(F32), jnp.where(even, pair, cross))
    for k, value in enumerate(frames):
        padded[PAD : PAD + POS, k * C1 : (k + 1) * C1] = value
        narrow = value.astype(BF16)
        for block in range(16):
            blocks_ref[block, CHUNK + k * POS : CHUNK + (k + 1) * POS] = narrow
    for row, col in TAPS9:
        step = PAD + COLS * (row - 1) + col - 1
        window = padded[step : step + POS]
        if col != 1:
            window = jnp.where(column_mask(col - 1, (POS, 3 * C1), 0), window, 0.0)
        moved[3 * row + col] = window.astype(BF16)
    slabs = []
    for slab in range(16):
        part = packed_ref[slab, 0:CHUNK].astype(F32)
        slabs.append(
            jnp.concatenate([part[8 * n : 8 * n + 8] for n in range(4 * CO // 128)], axis=1)
        )
    pix = jnp.concatenate(slabs, axis=0)
    center = pix - jnp.mean(pix, axis=-1, keepdims=True)
    spread = jnp.mean(center * center, axis=-1, keepdims=True)
    normed = center * lax.rsqrt(spread + 1e-06)
    spot = lax.broadcasted_iota(jnp.int32, (POS, index_ref.shape[1]), 0)
    hits = jnp.sum((spot == index_ref[...]).astype(F32), axis=1, keepdims=True)
    scale = (2.0 / (4 * CO)) * hits
    predict = jnp.zeros((4 * POS, CO), F32)
    for row, col in TAPS9:
        lhs = jnp.concatenate(
            [moved[3 * (token_step(i, row) + 1) + token_step(j, col) + 1] for i, j in PHASES], axis=0
        )
        predict = predict + jnp.dot(
            lhs, tap_weight(weight_ref, row, col), preferred_element_type=F32
        )
    predict = predict + bias_ref[...]
    turned = []
    for k in range(4):
        cot = scale * (predict[k * POS : (k + 1) * POS] - normed[:, k * CO : (k + 1) * CO])
        cot = cot.astype(BF16)
        cots[k * POS : (k + 1) * POS] = cot
        turned.append(cot.astype(F32).T)
    width = CO // 16
    for block in range(16):
        blocks_ref[block, 0:CHUNK] = jnp.concatenate(
            [part[block * width : (block + 1) * width] for part in turned], axis=0
        ).astype(BF16)

def back_conv(cots, weight_ref, to_pair_ref, keep_ref, to_cross_ref, shifted):
    even = lax.axis_index("seq") % 2 == 0
    zeros = jnp.zeros((PAD, 3 * C1), F32)
    cot = cots[...]
    sums = {}
    for row, col in TAPS9:
        part = lax.dot_general(
            cot, tap_weight(weight_ref, row, col), (((1,), (1,)), ((), ())),
            preferred_element_type=F32,
        )
        for k, (i, j) in enumerate(PHASES):
            key = (token_step(i, row), token_step(j, col))
            piece = part[k * POS : (k + 1) * POS]
            sums[key] = sums[key] + piece if key in sums else piece
    total = sums[(0, 0)]
    for k, ((row, col), value) in enumerate(sums.items()):
        if (row, col) == (0, 0):
            continue
        if col != 0:
            value = jnp.where(column_mask(col, (POS, 3 * C1), 0), value, 0.0)
        shifted[k, 0:PAD] = zeros
        shifted[k, PAD + POS :] = zeros
        shifted[k, PAD : PAD + POS] = value
        step = PAD - COLS * row - col
        total = total + shifted[k, step : step + POS]
    to_last, to_next = total[:, 0:C1], total[:, 2 * C1 :]
    to_pair_ref[...] = jnp.where(even, to_next, to_last)
    keep_ref[...] = total[:, C1 : 2 * C1]
    to_cross_ref[...] = jnp.where(even, to_last, to_next)


def halved(pairs, level, keep_ref, send_ref):
    bit = lax.axis_index("dp") // STEPS[level] % 2
    for at, (zero, one) in enumerate(pairs):
        keep_ref[at] = jnp.where(bit == 0, zero, one)
        send_ref[at] = jnp.where(bit == 0, one, zero).astype(send_ref.dtype)


def hidden_values(pair_ref, keep_ref, cross_ref, bias_ref, zsum_ref, hidden_ref):
    zsum = pair_ref[...] + keep_ref[...] + cross_ref[...] + bias_ref[...]
    zsum_ref[...] = zsum
    hidden_ref[...] = jax.nn.gelu(zsum, approximate=True).astype(BF16)


def hidden_grads(pair_ref, keep_ref, cross_ref, zsum_ref, out_ref):
    grad = pair_ref[...] + keep_ref[...] + cross_ref[...]
    gelu_tanh = partial(jax.nn.gelu, approximate=True)
    out_ref[...] = jax.vjp(gelu_tanh, zsum_ref[...])[1](grad)[0].astype(BF16)


def second_grads(blocks_ref, before_ref, out_ref, left, right):
    del before_ref
    wide, thin = CO // 16, C1 // 16
    masks = {}
    for row in (-1, 0, 1):
        for col in (-1, 0, 1):
            masks[(row, col)] = spot_mask(row, col, (1, POS), 1)
    for clip in range(16):
        lanes = slice(clip * POS, (clip + 1) * POS)
        value = blocks_ref[clip, 0:CHUNK].astype(F32)
        parts = []
        for row, i in PAIRS:
            for col, j in PAIRS:
                phase = 2 * i + j
                part = value[phase * wide : (phase + 1) * wide]
                step = COLS * row + col
                if step != 0:
                    part = pltpu.roll(part, (POS - step) % POS, 1)
                    part = jnp.where(masks[(row, col)], part, 0.0)
                parts.append(part)
        left[:, lanes] = jnp.concatenate(parts, axis=0).astype(BF16)
        for k in range(3):
            right[lanes, k * C1 : (k + 1) * C1] = blocks_ref[
                clip, CHUNK + k * POS : CHUNK + (k + 1) * POS
            ]
    both = jnp.dot(left[...], right[...], preferred_element_type=F32)
    parts = []
    for k in range(3):
        for row in range(3):
            for col in range(3):
                value = None
                for row_pair in PAIRS_OF_TAP[row]:
                    for col_pair in PAIRS_OF_TAP[col]:
                        at = (4 * PAIRS.index(row_pair) + PAIRS.index(col_pair)) * wide
                        piece = both[at : at + wide, k * C1 : (k + 1) * C1]
                        value = piece if value is None else value + piece
                parts.append(value)
    parts.append(jnp.zeros((6 * 128 - 27 * wide, C1), F32))
    turned = jnp.concatenate(parts, axis=0).T
    for block in range(16):
        two = turned[block * thin : (block + 1) * thin]
        out_ref[block] = jnp.concatenate(
            [two[:, 128 * n : 128 * (n + 1)] for n in range(6)], axis=0
        ).astype(out_ref.dtype)


def half_sum(level, kept_ref, came_ref, keep_ref, send_ref):
    pairs = [
        tuple(kept_ref[at] + came_ref[at].astype(F32) for at in (two, two + 1))
        for two in range(0, kept_ref.shape[0], 2)
    ]
    halved(pairs, level, keep_ref, send_ref)


def last_sum(kept_ref, came_ref, before_ref, out_ref):
    del before_ref
    total = kept_ref[0] + came_ref[0]
    width = out_ref.shape[2]
    for k in range(27):
        out_ref[k] = total[:, k * width : (k + 1) * width]


def first_grads(packed_ref, gz_ref, keep_ref, send_ref, moved):
    width, thin = D // 16, C1 // 16
    zeros = jnp.zeros((9 * width, POS), BF16)
    moved[:, 0:POS] = zeros
    moved[:, 17 * POS :] = zeros
    for frame in range(16):
        value = packed_ref[frame, CHUNK:].astype(F32)
        parts = []
        for row, col in TAPS9:
            part = value
            step = COLS * (row - 1) + col - 1
            if step != 0:
                part = pltpu.roll(value, (POS - step) % POS, 1)
                part = jnp.where(spot_mask(row - 1, col - 1, (1, POS), 1), part, 0.0)
            parts.append(part)
        moved[:, (frame + 1) * POS : (frame + 2) * POS] = jnp.concatenate(parts, axis=0).astype(
            BF16
        )
    right = gz_ref[...].reshape(16 * POS, C1)
    parts = []
    for k in range(3):
        parts.append(
            jnp.dot(moved[:, k * POS : (k + 16) * POS], right, preferred_element_type=F32)
        )
    parts.append(jnp.zeros((7 * 128 - 27 * width, C1), F32))
    turned = jnp.concatenate(parts, axis=0).T
    order = [sum(step for n, step in enumerate(STEPS) if slot >> n & 1) for slot in range(16)]
    blocks = [turned[block * thin : (block + 1) * thin] for block in order]
    halved(zip(blocks[0::2], blocks[1::2]), 0, keep_ref, send_ref)


def summed(parts_ref, out_ref):
    total = parts_ref[0].astype(F32)
    for source in range(1, 16):
        total = total + parts_ref[source].astype(F32)
    _, rows, width = out_ref.shape
    total = jnp.concatenate(
        [total[rows * n : rows * (n + 1)] for n in range(total.shape[0] // rows)], axis=1
    )
    for k in range(27):
        out_ref[k] = total[:, k * width : (k + 1) * width]


def exchange(value, axis):
    return lax.all_to_all(value, axis, split_axis=0, concat_axis=0, tiled=True)


def swapped(value, step, axis="seq"):
    return lax.ppermute(value, axis, [(i, i ^ step) for i in range(16)])


def with_pair(value):
    return swapped(value, 1)


def with_cross(value):
    swaps = [(i, i + 1) for i in range(1, 15, 2)]
    return lax.ppermute(value, "seq", swaps + [(j, i) for i, j in swaps])


def per_device(tokens, conv_first, bias_first, conv_second, bias_second, pixels, mask_index):
    packed, field = call(
        packed_inputs,
        (struct((16, CHUNK + D // 16, POS), BF16), struct((POS, D), BF16)),
        spots(pltpu.HBM, pltpu.HBM),
        [
            pltpu.VMEM((16, 2, 4, 4 * CO), BF16),
            pltpu.VMEM((32, 4, D), BF16),
            pltpu.SemaphoreType.DMA((2,)),
        ],
        flops=FLOPS // 10,
        limit=56,
    )(pixels[0], tokens[0, 0])
    plane = struct((POS, C1), F32)
    pair, keep, cross = call(
        first_conv,
        (plane, plane, plane),
        spots(VMEM, VMEM, pl.ANY),
        [pltpu.VMEM((POS + 2 * PAD, D), F32)],
    )(field, conv_first, packed)
    packed = exchange(packed, "seq")
    zsum, hidden = call(
        hidden_values,
        (plane, struct((POS, C1), BF16)),
        spots(*[VMEM] * 4),
        flops=FLOPS,
    )(with_pair(pair), keep, with_cross(cross), bias_first[None])

    blocks, cot = call(
        loss_cotangent,
        (struct((16, CHUNK + 3 * POS, POS), BF16), struct((4 * POS, CO), BF16)),
        spots(*[VMEM] * 7),
        [pltpu.VMEM((POS + 2 * PAD, 3 * C1), F32), pltpu.VMEM((9, POS, 3 * C1), BF16)],
    )(
        with_pair(hidden), hidden, with_cross(hidden), conv_second, bias_second[None],
        packed, mask_index,
    )
    pair, keep, cross = call(
        back_conv,
        (plane, plane, plane),
        spots(VMEM, VMEM),
        [pltpu.VMEM((9, POS + 2 * PAD, 3 * C1), F32)],
        size=4 << 20,
    )(cot, conv_second)
    blocks = exchange(blocks, "dp")
    grad_z = call(hidden_grads, struct((POS, C1), BF16), spots(*[VMEM] * 4))(
        with_pair(pair), keep, with_cross(cross), zsum
    )
    grad_z = lax.all_gather(grad_z, "seq")

    half = struct((8, C1 // 16, 7 * 128), F32)
    keep, send = call(
        first_grads,
        (half, half),
        spots(VMEM, VMEM),
        [pltpu.VMEM((9 * D // 16, 18 * POS), BF16)],
    )(packed, grad_z)
    grad_first_half = keep
    for level in (1, 2, 3):
        half = struct((8 >> level, C1 // 16, 7 * 128), F32)
        came = swapped(send, STEPS[level - 1], "dp")
        sent = struct(half.shape, BF16 if level == 1 else F32)
        keep, send = call(
            partial(half_sum, level), (half, sent), spots(VMEM, VMEM)
        )(keep, came)
    second = call(
        second_grads,
        struct((16, 48, 128), BF16),
        spots(VMEM, pl.ANY),
        [pltpu.VMEM((CO, 16 * POS), BF16), pltpu.VMEM((16 * POS, CO), BF16)],
        size=4 << 20,
    )(blocks, grad_first_half)
    grad_second = call(summed, struct((27, C1 // 16, CO // 16), F32), spots(VMEM))(
        exchange(second, "seq")
    )
    grad_second = grad_second.transpose(1, 2, 0)
    grad_first = call(last_sum, struct((27, C1 // 16, D // 16), F32), spots(VMEM, VMEM, pl.ANY))(
        keep, swapped(send, STEPS[3], "dp"), grad_second
    )
    return grad_first.transpose(0, 2, 1), grad_second.transpose(2, 0, 1)


def solution(mesh):
    return jax.shard_map(
        per_device,
        mesh=mesh,
        in_specs=(
            P("dp", "seq", None, None, None),
            P(),
            P(),
            P(),
            P(),
            P("dp", None, "seq", None, None),
            P("dp", None),
        ),
        out_specs=(P(None, "seq", "dp"), P(None, "seq", "dp")),
        check_vma=False,
    )
```

```python
from functools import partial

import jax
import jax.numpy as jnp
from jax import lax
from jax.experimental import pallas as pl
from jax.experimental.pallas import tpu as pltpu
from jax.sharding import PartitionSpec as P

F32 = jnp.float32
BF16 = jnp.bfloat16
POS, COLS, PAD = 128, 4, 8
D, C1, CO = 512, 128, 384
CHUNK = 4 * CO // 16
FLOPS = 40_000_000_000
STEPS = (2, 1, 8, 4)
TAPS9 = [(row, col) for row in range(3) for col in range(3)]
PHASES = [(i, j) for i in range(2) for j in range(2)]
PAIRS = [(-1, 1), (0, 0), (0, 1), (1, 0)]
PAIRS_OF_TAP = [[(0, 1), (1, 0)], [(0, 0), (0, 1)], [(-1, 1), (0, 0)]]


def token_step(phase, tap):
    return (phase + tap - 1) // 2


def column_mask(step, shape, axis):
    column = lax.broadcasted_iota(jnp.int32, shape, axis) % COLS + step
    return (column >= 0) & (column < COLS)


def spot_mask(row_step, col_step, shape, axis):
    spot = lax.broadcasted_iota(jnp.int32, shape, axis)
    column = spot % COLS + col_step
    row = spot // COLS + row_step
    return (column >= 0) & (column < COLS) & (row >= 0) & (row < POS // COLS)


def call(body, out_shape, in_specs, scratch=(), flops=0, size=0, limit=16, **options):
    return pl.pallas_call(
        body,
        out_shape=out_shape,
        in_specs=in_specs,
        **options,
        scratch_shapes=list(scratch),
        compiler_params=pltpu.CompilerParams(vmem_limit_bytes=limit << 20),
        cost_estimate=pl.CostEstimate(flops=flops, bytes_accessed=size, transcendentals=0),
    )


def struct(shape, dtype):
    return jax.ShapeDtypeStruct(shape, dtype)


VMEM = pltpu.VMEM


def spots(*kinds):
    return [pl.BlockSpec(memory_space=kind) for kind in kinds]


def packed_and_convolved(pixel_source, tokens_source, weight_source,
                         out_ref, pair_ref, keep_ref, cross_ref,
                         pixel_ref, tokens_ref, weight_ref, padded, sems):
    copies = [
        pltpu.make_async_copy(source, target, sems.at[n])
        for n, (source, target) in enumerate(
            (
                (tokens_source, tokens_ref),
                (pixel_source, pixel_ref),
                (weight_source, weight_ref),
            )
        )
    ]
    for copy in copies:
        copy.start()
    copies[0].wait()
    tokens = tokens_ref[...].astype(F32).reshape(POS, D)
    padded[PAD : PAD + POS] = tokens
    tokens = tokens.astype(BF16)
    turned = tokens.T
    width = D // 16
    copies[1].wait()
    for block in range(16):
        pix = pixel_ref[block].astype(F32).reshape(8, 4 * CO)
        out_ref[block, 0:CHUNK] = jnp.concatenate(
            [pix[:, n * 128 : (n + 1) * 128] for n in range(4 * CO // 128)], axis=0
        ).astype(BF16)
        out_ref[block, CHUNK:] = turned[block * width : (block + 1) * width]
    padded[0:PAD] = jnp.zeros((PAD, D), F32)
    padded[PAD + POS :] = jnp.zeros((PAD, D), F32)
    copies[2].wait()
    total = jnp.zeros((POS, 3 * C1), F32)
    for row, col in TAPS9:
        step = PAD + COLS * (row - 1) + col - 1
        window = padded[step : step + POS]
        if col != 1:
            window = jnp.where(column_mask(col - 1, (POS, D), 0), window, 0.0)
        tap = 3 * row + col
        weight = jnp.concatenate([weight_ref[tap + 9 * k] for k in range(3)], axis=1)
        total = total + jnp.dot(window.astype(BF16), weight, preferred_element_type=F32)
    to_next, to_last = total[:, 0:C1], total[:, 2 * C1 :]
    even = lax.axis_index("seq") % 2 == 0
    pair_ref[...] = jnp.where(even, to_next, to_last)
    keep_ref[...] = total[:, C1 : 2 * C1]
    cross_ref[...] = jnp.where(even, to_last, to_next)


def tap_weight(weight_ref, row, col):
    return jnp.concatenate([weight_ref[9 * k + 3 * row + col] for k in range(3)], axis=0)


def loss_cotangent(pair_ref, here_ref, cross_ref, weight_ref, bias_ref, packed_ref,
                   index_ref, blocks_ref, cots, padded, moved):
    even = lax.axis_index("seq") % 2 == 0
    zeros = jnp.zeros((PAD, 3 * C1), F32)
    padded[0:PAD] = zeros
    padded[PAD + POS :] = zeros
    pair, cross = pair_ref[...].astype(F32), cross_ref[...].astype(F32)
    frames = (jnp.where(even, cross, pair), here_ref[...].astype(F32), jnp.where(even, pair, cross))
    for k, value in enumerate(frames):
        padded[PAD : PAD + POS, k * C1 : (k + 1) * C1] = value
        narrow = value.astype(BF16)
        for block in range(16):
            blocks_ref[block, CHUNK + k * POS : CHUNK + (k + 1) * POS] = narrow
    for row, col in TAPS9:
        step = PAD + COLS * (row - 1) + col - 1
        window = padded[step : step + POS]
        if col != 1:
            window = jnp.where(column_mask(col - 1, (POS, 3 * C1), 0), window, 0.0)
        moved[3 * row + col] = window.astype(BF16)
    slabs = []
    for slab in range(16):
        part = packed_ref[slab, 0:CHUNK].astype(F32)
        slabs.append(
            jnp.concatenate([part[8 * n : 8 * n + 8] for n in range(4 * CO // 128)], axis=1)
        )
    pix = jnp.concatenate(slabs, axis=0)
    center = pix - jnp.mean(pix, axis=-1, keepdims=True)
    spread = jnp.mean(center * center, axis=-1, keepdims=True)
    normed = center * lax.rsqrt(spread + 1e-06)
    spot = lax.broadcasted_iota(jnp.int32, (POS, index_ref.shape[1]), 0)
    hits = jnp.sum((spot == index_ref[...]).astype(F32), axis=1, keepdims=True)
    scale = (2.0 / (4 * CO)) * hits
    predict = jnp.zeros((4 * POS, CO), F32)
    for row, col in TAPS9:
        lhs = jnp.concatenate(
            [moved[3 * (token_step(i, row) + 1) + token_step(j, col) + 1] for i, j in PHASES], axis=0
        )
        predict = predict + jnp.dot(
            lhs, tap_weight(weight_ref, row, col), preferred_element_type=F32
        )
    predict = predict + bias_ref[...]
    turned = []
    for k in range(4):
        cot = scale * (predict[k * POS : (k + 1) * POS] - normed[:, k * CO : (k + 1) * CO])
        cot = cot.astype(BF16)
        cots[k * POS : (k + 1) * POS] = cot
        turned.append(cot.astype(F32).T)
    width = CO // 16
    for block in range(16):
        blocks_ref[block, 0:CHUNK] = jnp.concatenate(
            [part[block * width : (block + 1) * width] for part in turned], axis=0
        ).astype(BF16)

def back_conv(cots, weight_ref, to_pair_ref, keep_ref, to_cross_ref, shifted):
    even = lax.axis_index("seq") % 2 == 0
    zeros = jnp.zeros((PAD, 3 * C1), F32)
    cot = cots[...]
    sums = {}
    for row, col in TAPS9:
        part = lax.dot_general(
            cot, tap_weight(weight_ref, row, col), (((1,), (1,)), ((), ())),
            preferred_element_type=F32,
        )
        for k, (i, j) in enumerate(PHASES):
            key = (token_step(i, row), token_step(j, col))
            piece = part[k * POS : (k + 1) * POS]
            sums[key] = sums[key] + piece if key in sums else piece
    total = sums[(0, 0)]
    for k, ((row, col), value) in enumerate(sums.items()):
        if (row, col) == (0, 0):
            continue
        if col != 0:
            value = jnp.where(column_mask(col, (POS, 3 * C1), 0), value, 0.0)
        shifted[k, 0:PAD] = zeros
        shifted[k, PAD + POS :] = zeros
        shifted[k, PAD : PAD + POS] = value
        step = PAD - COLS * row - col
        total = total + shifted[k, step : step + POS]
    to_last, to_next = total[:, 0:C1], total[:, 2 * C1 :]
    to_pair_ref[...] = jnp.where(even, to_next, to_last)
    keep_ref[...] = total[:, C1 : 2 * C1]
    to_cross_ref[...] = jnp.where(even, to_last, to_next)


def halved(pairs, level, keep_ref, send_ref):
    bit = lax.axis_index("dp") // STEPS[level] % 2
    for at, (zero, one) in enumerate(pairs):
        keep_ref[at] = jnp.where(bit == 0, zero, one)
        send_ref[at] = jnp.where(bit == 0, one, zero).astype(send_ref.dtype)


def hidden_values(pair_ref, keep_ref, cross_ref, bias_ref, zsum_ref, hidden_ref):
    zsum = pair_ref[...] + keep_ref[...] + cross_ref[...] + bias_ref[...]
    zsum_ref[...] = zsum
    hidden_ref[...] = jax.nn.gelu(zsum, approximate=True).astype(BF16)


def hidden_grads(pair_ref, keep_ref, cross_ref, zsum_ref, out_ref):
    grad = pair_ref[...] + keep_ref[...] + cross_ref[...]
    gelu_tanh = partial(jax.nn.gelu, approximate=True)
    out_ref[...] = jax.vjp(gelu_tanh, zsum_ref[...])[1](grad)[0].astype(BF16)


def second_grads(blocks_ref, before_ref, out_ref, left, right):
    del before_ref
    wide, thin = CO // 16, C1 // 16
    masks = {}
    for row in (-1, 0, 1):
        for col in (-1, 0, 1):
            masks[(row, col)] = spot_mask(row, col, (1, POS), 1)
    for clip in range(16):
        lanes = slice(clip * POS, (clip + 1) * POS)
        value = blocks_ref[clip, 0:CHUNK].astype(F32)
        parts = []
        for row, i in PAIRS:
            for col, j in PAIRS:
                phase = 2 * i + j
                part = value[phase * wide : (phase + 1) * wide]
                step = COLS * row + col
                if step != 0:
                    part = pltpu.roll(part, (POS - step) % POS, 1)
                    part = jnp.where(masks[(row, col)], part, 0.0)
                parts.append(part)
        left[:, lanes] = jnp.concatenate(parts, axis=0).astype(BF16)
        for k in range(3):
            right[lanes, k * C1 : (k + 1) * C1] = blocks_ref[
                clip, CHUNK + k * POS : CHUNK + (k + 1) * POS
            ]
    both = jnp.dot(left[...], right[...], preferred_element_type=F32)
    parts = []
    for k in range(3):
        for row in range(3):
            for col in range(3):
                value = None
                for row_pair in PAIRS_OF_TAP[row]:
                    for col_pair in PAIRS_OF_TAP[col]:
                        at = (4 * PAIRS.index(row_pair) + PAIRS.index(col_pair)) * wide
                        piece = both[at : at + wide, k * C1 : (k + 1) * C1]
                        value = piece if value is None else value + piece
                parts.append(value)
    parts.append(jnp.zeros((6 * 128 - 27 * wide, C1), F32))
    turned = jnp.concatenate(parts, axis=0).T
    for block in range(16):
        two = turned[block * thin : (block + 1) * thin]
        out_ref[block] = jnp.concatenate(
            [two[:, 128 * n : 128 * (n + 1)] for n in range(6)], axis=0
        ).astype(out_ref.dtype)


def half_sum(level, kept_ref, came_ref, keep_ref, send_ref):
    pairs = [
        tuple(kept_ref[at] + came_ref[at].astype(F32) for at in (two, two + 1))
        for two in range(0, kept_ref.shape[0], 2)
    ]
    halved(pairs, level, keep_ref, send_ref)


def last_sum(kept_ref, came_ref, before_ref, out_ref):
    del before_ref
    total = kept_ref[0] + came_ref[0]
    width = out_ref.shape[2]
    for k in range(27):
        out_ref[k] = total[:, k * width : (k + 1) * width]


def first_grads(packed_ref, gz_ref, keep_ref, send_ref, moved):
    width, thin = D // 16, C1 // 16
    zeros = jnp.zeros((9 * width, POS), BF16)
    moved[:, 0:POS] = zeros
    moved[:, 17 * POS :] = zeros
    for frame in range(16):
        value = packed_ref[frame, CHUNK:].astype(F32)
        parts = []
        for row, col in TAPS9:
            part = value
            step = COLS * (row - 1) + col - 1
            if step != 0:
                part = pltpu.roll(value, (POS - step) % POS, 1)
                part = jnp.where(spot_mask(row - 1, col - 1, (1, POS), 1), part, 0.0)
            parts.append(part)
        moved[:, (frame + 1) * POS : (frame + 2) * POS] = jnp.concatenate(parts, axis=0).astype(
            BF16
        )
    right = gz_ref[...].reshape(16 * POS, C1)
    parts = []
    for k in range(3):
        parts.append(
            jnp.dot(moved[:, k * POS : (k + 16) * POS], right, preferred_element_type=F32)
        )
    parts.append(jnp.zeros((7 * 128 - 27 * width, C1), F32))
    turned = jnp.concatenate(parts, axis=0).T
    order = [sum(step for n, step in enumerate(STEPS) if slot >> n & 1) for slot in range(16)]
    blocks = [turned[block * thin : (block + 1) * thin] for block in order]
    halved(zip(blocks[0::2], blocks[1::2]), 0, keep_ref, send_ref)


def summed(parts_ref, out_ref):
    total = parts_ref[0].astype(F32)
    for source in range(1, 16):
        total = total + parts_ref[source].astype(F32)
    _, rows, width = out_ref.shape
    total = jnp.concatenate(
        [total[rows * n : rows * (n + 1)] for n in range(total.shape[0] // rows)], axis=1
    )
    for k in range(27):
        out_ref[k] = total[:, k * width : (k + 1) * width]


def exchange(value, axis):
    return lax.all_to_all(value, axis, split_axis=0, concat_axis=0, tiled=True)


def swapped(value, step, axis="seq"):
    return lax.ppermute(value, axis, [(i, i ^ step) for i in range(16)])


def with_pair(value):
    return swapped(value, 1)


def with_cross(value):
    swaps = [(i, i + 1) for i in range(1, 15, 2)]
    return lax.ppermute(value, "seq", swaps + [(j, i) for i, j in swaps])


def per_device(tokens, conv_first, bias_first, conv_second, bias_second, pixels, mask_index):
    plane = struct((POS, C1), F32)
    packed, pair, keep, cross = call(
        packed_and_convolved,
        (struct((16, CHUNK + D // 16, POS), BF16), plane, plane, plane),
        spots(pltpu.HBM, pltpu.HBM, pltpu.HBM),
        [
            pltpu.VMEM((16, 2, 4, 4 * CO), BF16),
            pltpu.VMEM((32, 4, D), BF16),
            pltpu.VMEM((27, D, C1), BF16),
            pltpu.VMEM((POS + 2 * PAD, D), F32),
            pltpu.SemaphoreType.DMA((3,)),
        ],
        limit=60,
    )(pixels[0], tokens[0, 0], conv_first)
    packed = exchange(packed, "seq")
    zsum, hidden = call(
        hidden_values,
        (plane, struct((POS, C1), BF16)),
        spots(*[VMEM] * 4),
        flops=FLOPS,
    )(with_pair(pair), keep, with_cross(cross), bias_first[None])

    blocks, cot = call(
        loss_cotangent,
        (struct((16, CHUNK + 3 * POS, POS), BF16), struct((4 * POS, CO), BF16)),
        spots(*[VMEM] * 7),
        [pltpu.VMEM((POS + 2 * PAD, 3 * C1), F32), pltpu.VMEM((9, POS, 3 * C1), BF16)],
    )(
        with_pair(hidden), hidden, with_cross(hidden), conv_second, bias_second[None],
        packed, mask_index,
    )
    pair, keep, cross = call(
        back_conv,
        (plane, plane, plane),
        spots(VMEM, VMEM),
        [pltpu.VMEM((9, POS + 2 * PAD, 3 * C1), F32)],
        size=4 << 20,
    )(cot, conv_second)
    blocks = exchange(blocks, "dp")
    grad_z = call(hidden_grads, struct((POS, C1), BF16), spots(*[VMEM] * 4))(
        with_pair(pair), keep, with_cross(cross), zsum
    )
    grad_z = lax.all_gather(grad_z, "seq")

    half = struct((8, C1 // 16, 7 * 128), F32)
    keep, send = call(
        first_grads,
        (half, half),
        spots(VMEM, VMEM),
        [pltpu.VMEM((9 * D // 16, 18 * POS), BF16)],
    )(packed, grad_z)
    grad_first_half = keep
    for level in (1, 2, 3):
        half = struct((8 >> level, C1 // 16, 7 * 128), F32)
        came = swapped(send, STEPS[level - 1], "dp")
        sent = struct(half.shape, BF16 if level == 1 else F32)
        keep, send = call(
            partial(half_sum, level), (half, sent), spots(VMEM, VMEM)
        )(keep, came)
    second = call(
        second_grads,
        struct((16, 48, 128), BF16),
        spots(VMEM, pl.ANY),
        [pltpu.VMEM((CO, 16 * POS), BF16), pltpu.VMEM((16 * POS, CO), BF16)],
        size=4 << 20,
    )(blocks, grad_first_half)
    grad_second = call(summed, struct((27, C1 // 16, CO // 16), F32), spots(VMEM))(
        exchange(second, "seq")
    )
    grad_second = grad_second.transpose(1, 2, 0)
    grad_first = call(last_sum, struct((27, C1 // 16, D // 16), F32), spots(VMEM, VMEM, pl.ANY))(
        keep, swapped(send, STEPS[3], "dp"), grad_second
    )
    return grad_first.transpose(0, 2, 1), grad_second.transpose(2, 0, 1)


def solution(mesh):
    return jax.shard_map(
        per_device,
        mesh=mesh,
        in_specs=(
            P("dp", "seq", None, None, None),
            P(),
            P(),
            P(),
            P(),
            P("dp", None, "seq", None, None),
            P("dp", None),
        ),
        out_specs=(P(None, "seq", "dp"), P(None, "seq", "dp")),
        check_vma=False,
    )
```

```python
from functools import partial

import jax
import jax.numpy as jnp
from jax import lax
from jax.experimental import pallas as pl
from jax.experimental.pallas import tpu as pltpu
from jax.sharding import PartitionSpec as P

F32 = jnp.float32
BF16 = jnp.bfloat16
POS, COLS, PAD = 128, 4, 8
D, C1, CO = 512, 128, 384
CHUNK = 4 * CO // 16
FLOPS = 40_000_000_000
STEPS = (2, 1, 8, 4)
TAPS9 = [(row, col) for row in range(3) for col in range(3)]
PHASES = [(i, j) for i in range(2) for j in range(2)]
PAIRS = [(-1, 1), (0, 0), (0, 1), (1, 0)]
PAIRS_OF_TAP = [[(0, 1), (1, 0)], [(0, 0), (0, 1)], [(-1, 1), (0, 0)]]


def token_step(phase, tap):
    return (phase + tap - 1) // 2


def column_mask(step, shape, axis):
    column = lax.broadcasted_iota(jnp.int32, shape, axis) % COLS + step
    return (column >= 0) & (column < COLS)


def spot_mask(row_step, col_step, shape, axis):
    spot = lax.broadcasted_iota(jnp.int32, shape, axis)
    column = spot % COLS + col_step
    row = spot // COLS + row_step
    return (column >= 0) & (column < COLS) & (row >= 0) & (row < POS // COLS)


def call(body, out_shape, in_specs, scratch=(), flops=0, size=0, limit=16, **options):
    return pl.pallas_call(
        body,
        out_shape=out_shape,
        in_specs=in_specs,
        **options,
        scratch_shapes=list(scratch),
        compiler_params=pltpu.CompilerParams(vmem_limit_bytes=limit << 20),
        cost_estimate=pl.CostEstimate(flops=flops, bytes_accessed=size, transcendentals=0),
    )


def struct(shape, dtype):
    return jax.ShapeDtypeStruct(shape, dtype)


VMEM = pltpu.VMEM


def spots(*kinds):
    return [pl.BlockSpec(memory_space=kind) for kind in kinds]


def packed_and_convolved(pixel_source, tokens_source, weight_source,
                         out_ref, pair_ref, keep_ref, cross_ref,
                         pixel_ref, tokens_ref, weight_ref, padded, sems):
    copies = [
        pltpu.make_async_copy(source, target, sems.at[n])
        for n, (source, target) in enumerate(
            (
                (tokens_source, tokens_ref),
                (pixel_source, pixel_ref),
                (weight_source, weight_ref),
            )
        )
    ]
    for copy in copies:
        copy.start()
    copies[0].wait()
    tokens = tokens_ref[...].astype(F32).reshape(POS, D)
    padded[PAD : PAD + POS] = tokens
    tokens = tokens.astype(BF16)
    turned = tokens.T
    width = D // 16
    copies[1].wait()
    for block in range(16):
        pix = pixel_ref[block].astype(F32).reshape(8, 4 * CO)
        out_ref[block, 0:CHUNK] = jnp.concatenate(
            [pix[:, n * 128 : (n + 1) * 128] for n in range(4 * CO // 128)], axis=0
        ).astype(BF16)
        out_ref[block, CHUNK:] = turned[block * width : (block + 1) * width]
    padded[0:PAD] = jnp.zeros((PAD, D), F32)
    padded[PAD + POS :] = jnp.zeros((PAD, D), F32)
    copies[2].wait()
    total = jnp.zeros((POS, 3 * C1), F32)
    for row, col in TAPS9:
        step = PAD + COLS * (row - 1) + col - 1
        window = padded[step : step + POS]
        if col != 1:
            window = jnp.where(column_mask(col - 1, (POS, D), 0), window, 0.0)
        tap = 3 * row + col
        weight = jnp.concatenate([weight_ref[tap + 9 * k] for k in range(3)], axis=1)
        total = total + jnp.dot(window.astype(BF16), weight, preferred_element_type=F32)
    to_next, to_last = total[:, 0:C1], total[:, 2 * C1 :]
    even = lax.axis_index("seq") % 2 == 0
    pair_ref[...] = jnp.where(even, to_next, to_last)
    keep_ref[...] = total[:, C1 : 2 * C1]
    cross_ref[...] = jnp.where(even, to_last, to_next)


def tap_weight(weight_ref, row, col):
    return jnp.concatenate([weight_ref[9 * k + 3 * row + col] for k in range(3)], axis=0)


def loss_cotangent(pair_ref, here_ref, cross_ref, weight_ref, bias_ref, packed_ref,
                   index_ref, blocks_ref, cots, padded, moved):
    even = lax.axis_index("seq") % 2 == 0
    zeros = jnp.zeros((PAD, 3 * C1), F32)
    padded[0:PAD] = zeros
    padded[PAD + POS :] = zeros
    pair, cross = pair_ref[...].astype(F32), cross_ref[...].astype(F32)
    frames = (jnp.where(even, cross, pair), here_ref[...].astype(F32), jnp.where(even, pair, cross))
    for k, value in enumerate(frames):
        padded[PAD : PAD + POS, k * C1 : (k + 1) * C1] = value
        narrow = value.astype(BF16)
        for block in range(16):
            blocks_ref[block, CHUNK + k * POS : CHUNK + (k + 1) * POS] = narrow
    for row, col in TAPS9:
        step = PAD + COLS * (row - 1) + col - 1
        window = padded[step : step + POS]
        if col != 1:
            window = jnp.where(column_mask(col - 1, (POS, 3 * C1), 0), window, 0.0)
        moved[3 * row + col] = window.astype(BF16)
    slabs = []
    for slab in range(16):
        part = packed_ref[slab, 0:CHUNK].astype(F32)
        slabs.append(
            jnp.concatenate([part[8 * n : 8 * n + 8] for n in range(4 * CO // 128)], axis=1)
        )
    pix = jnp.concatenate(slabs, axis=0)
    center = pix - jnp.mean(pix, axis=-1, keepdims=True)
    spread = jnp.mean(center * center, axis=-1, keepdims=True)
    normed = center * lax.rsqrt(spread + 1e-06)
    spot = lax.broadcasted_iota(jnp.int32, (POS, index_ref.shape[1]), 0)
    hits = jnp.sum((spot == index_ref[...]).astype(F32), axis=1, keepdims=True)
    scale = (2.0 / (4 * CO)) * hits
    predict = jnp.zeros((4 * POS, CO), F32)
    for row, col in TAPS9:
        lhs = jnp.concatenate(
            [moved[3 * (token_step(i, row) + 1) + token_step(j, col) + 1] for i, j in PHASES], axis=0
        )
        predict = predict + jnp.dot(
            lhs, tap_weight(weight_ref, row, col), preferred_element_type=F32
        )
    predict = predict + bias_ref[...]
    turned = []
    for k in range(4):
        cot = scale * (predict[k * POS : (k + 1) * POS] - normed[:, k * CO : (k + 1) * CO])
        cot = cot.astype(BF16)
        cots[k * POS : (k + 1) * POS] = cot
        turned.append(cot.astype(F32).T)
    width = CO // 16
    for block in range(16):
        blocks_ref[block, 0:CHUNK] = jnp.concatenate(
            [part[block * width : (block + 1) * width] for part in turned], axis=0
        ).astype(BF16)

def back_conv(cots, weight_ref, to_pair_ref, keep_ref, to_cross_ref, shifted):
    even = lax.axis_index("seq") % 2 == 0
    zeros = jnp.zeros((PAD, 3 * C1), F32)
    cot = cots[...]
    sums = {}
    for row, col in TAPS9:
        part = lax.dot_general(
            cot, tap_weight(weight_ref, row, col), (((1,), (1,)), ((), ())),
            preferred_element_type=F32,
        )
        for k, (i, j) in enumerate(PHASES):
            key = (token_step(i, row), token_step(j, col))
            piece = part[k * POS : (k + 1) * POS]
            sums[key] = sums[key] + piece if key in sums else piece
    total = sums[(0, 0)]
    for k, ((row, col), value) in enumerate(sums.items()):
        if (row, col) == (0, 0):
            continue
        if col != 0:
            value = jnp.where(column_mask(col, (POS, 3 * C1), 0), value, 0.0)
        shifted[k, 0:PAD] = zeros
        shifted[k, PAD + POS :] = zeros
        shifted[k, PAD : PAD + POS] = value
        step = PAD - COLS * row - col
        total = total + shifted[k, step : step + POS]
    to_last, to_next = total[:, 0:C1], total[:, 2 * C1 :]
    to_pair_ref[...] = jnp.where(even, to_next, to_last)
    keep_ref[...] = total[:, C1 : 2 * C1]
    to_cross_ref[...] = jnp.where(even, to_last, to_next)


def halved(pairs, level, keep_ref, send_ref):
    bit = lax.axis_index("dp") // STEPS[level] % 2
    for at, (zero, one) in enumerate(pairs):
        keep_ref[at] = jnp.where(bit == 0, zero, one)
        send_ref[at] = jnp.where(bit == 0, one, zero).astype(send_ref.dtype)


def hidden_values(pair_ref, keep_ref, cross_ref, bias_ref, zsum_ref, hidden_ref):
    zsum = pair_ref[...] + keep_ref[...] + cross_ref[...] + bias_ref[...]
    zsum_ref[...] = zsum
    hidden_ref[...] = jax.nn.gelu(zsum, approximate=True).astype(BF16)


def hidden_grads(pair_ref, keep_ref, cross_ref, zsum_ref, out_ref):
    grad = pair_ref[...] + keep_ref[...] + cross_ref[...]
    gelu_tanh = partial(jax.nn.gelu, approximate=True)
    out_ref[...] = jax.vjp(gelu_tanh, zsum_ref[...])[1](grad)[0].astype(BF16)


def second_grads(blocks_ref, before_ref, out_ref, left, right):
    del before_ref
    wide, thin = CO // 16, C1 // 16
    masks = {}
    for row in (-1, 0, 1):
        for col in (-1, 0, 1):
            masks[(row, col)] = spot_mask(row, col, (1, POS), 1)
    for clip in range(16):
        lanes = slice(clip * POS, (clip + 1) * POS)
        value = blocks_ref[clip, 0:CHUNK].astype(F32)
        parts = []
        for row, i in PAIRS:
            for col, j in PAIRS:
                phase = 2 * i + j
                part = value[phase * wide : (phase + 1) * wide]
                step = COLS * row + col
                if step != 0:
                    part = pltpu.roll(part, (POS - step) % POS, 1)
                    part = jnp.where(masks[(row, col)], part, 0.0)
                parts.append(part)
        left[:, lanes] = jnp.concatenate(parts, axis=0).astype(BF16)
        for k in range(3):
            right[lanes, k * C1 : (k + 1) * C1] = blocks_ref[
                clip, CHUNK + k * POS : CHUNK + (k + 1) * POS
            ]
    both = jnp.dot(left[...], right[...], preferred_element_type=F32)
    parts = []
    for k in range(3):
        for row in range(3):
            for col in range(3):
                value = None
                for row_pair in PAIRS_OF_TAP[row]:
                    for col_pair in PAIRS_OF_TAP[col]:
                        at = (4 * PAIRS.index(row_pair) + PAIRS.index(col_pair)) * wide
                        piece = both[at : at + wide, k * C1 : (k + 1) * C1]
                        value = piece if value is None else value + piece
                parts.append(value)
    parts.append(jnp.zeros((6 * 128 - 27 * wide, C1), F32))
    turned = jnp.concatenate(parts, axis=0).T
    for block in range(16):
        two = turned[block * thin : (block + 1) * thin]
        out_ref[block] = jnp.concatenate(
            [two[:, 128 * n : 128 * (n + 1)] for n in range(6)], axis=0
        ).astype(out_ref.dtype)


def half_sum(level, kept_ref, came_ref, keep_ref, send_ref):
    pairs = [
        tuple(kept_ref[at] + came_ref[at].astype(F32) for at in (two, two + 1))
        for two in range(0, kept_ref.shape[0], 2)
    ]
    halved(pairs, level, keep_ref, send_ref)


def last_sum(kept_ref, came_ref, before_ref, out_ref):
    del before_ref
    total = kept_ref[0] + came_ref[0]
    width = out_ref.shape[2]
    for k in range(27):
        out_ref[k] = total[:, k * width : (k + 1) * width]


def first_grads(packed_ref, gz_ref, keep_ref, send_ref, moved):
    width, thin = D // 16, C1 // 16
    zeros = jnp.zeros((9 * width, POS), BF16)
    moved[:, 0:POS] = zeros
    moved[:, 17 * POS :] = zeros
    for frame in range(16):
        value = packed_ref[frame, CHUNK:].astype(F32)
        parts = []
        for row, col in TAPS9:
            part = value
            step = COLS * (row - 1) + col - 1
            if step != 0:
                part = pltpu.roll(value, (POS - step) % POS, 1)
                part = jnp.where(spot_mask(row - 1, col - 1, (1, POS), 1), part, 0.0)
            parts.append(part)
        moved[:, (frame + 1) * POS : (frame + 2) * POS] = jnp.concatenate(parts, axis=0).astype(
            BF16
        )
    right = gz_ref[...].reshape(16 * POS, C1)
    parts = []
    for k in range(3):
        parts.append(
            jnp.dot(moved[:, k * POS : (k + 16) * POS], right, preferred_element_type=F32)
        )
    parts.append(jnp.zeros((7 * 128 - 27 * width, C1), F32))
    turned = jnp.concatenate(parts, axis=0).T
    order = [sum(step for n, step in enumerate(STEPS) if slot >> n & 1) for slot in range(16)]
    blocks = [turned[block * thin : (block + 1) * thin] for block in order]
    halved(zip(blocks[0::2], blocks[1::2]), 0, keep_ref, send_ref)


def summed(parts_ref, out_ref):
    total = parts_ref[0].astype(F32)
    for source in range(1, 16):
        total = total + parts_ref[source].astype(F32)
    _, rows, width = out_ref.shape
    total = jnp.concatenate(
        [total[rows * n : rows * (n + 1)] for n in range(total.shape[0] // rows)], axis=1
    )
    for k in range(27):
        out_ref[k] = total[:, k * width : (k + 1) * width]


def exchange(value, axis):
    return lax.all_to_all(value, axis, split_axis=0, concat_axis=0, tiled=True)


def swapped(value, step, axis="seq"):
    return lax.ppermute(value, axis, [(i, i ^ step) for i in range(16)])


def with_pair(value):
    return swapped(value, 1)


def with_cross(value):
    swaps = [(i, i + 1) for i in range(1, 15, 2)]
    return lax.ppermute(value, "seq", swaps + [(j, i) for i, j in swaps])


def per_device(tokens, conv_first, bias_first, conv_second, bias_second, pixels, mask_index):
    plane = struct((POS, C1), F32)
    packed, pair, keep, cross = call(
        packed_and_convolved,
        (struct((16, CHUNK + D // 16, POS), BF16), plane, plane, plane),
        spots(pltpu.HBM, pltpu.HBM, pltpu.HBM),
        [
            pltpu.VMEM((16, 2, 4, 4 * CO), BF16),
            pltpu.VMEM((32, 4, D), BF16),
            pltpu.VMEM((27, D, C1), BF16),
            pltpu.VMEM((POS + 2 * PAD, D), F32),
            pltpu.SemaphoreType.DMA((3,)),
        ],
        limit=60,
    )(pixels[0], tokens[0, 0], conv_first)
    packed = exchange(packed, "seq")
    zsum, hidden = call(
        hidden_values,
        (plane, struct((POS, C1), BF16)),
        spots(*[VMEM] * 4),
        flops=FLOPS,
    )(with_pair(pair), keep, with_cross(cross), bias_first[None])

    blocks, cot = call(
        loss_cotangent,
        (struct((16, CHUNK + 3 * POS, POS), BF16), struct((4 * POS, CO), BF16)),
        spots(*[VMEM] * 7),
        [pltpu.VMEM((POS + 2 * PAD, 3 * C1), F32), pltpu.VMEM((9, POS, 3 * C1), BF16)],
    )(
        with_pair(hidden), hidden, with_cross(hidden), conv_second, bias_second[None],
        packed, mask_index,
    )
    pair, keep, cross = call(
        back_conv,
        (plane, plane, plane),
        spots(VMEM, VMEM),
        [pltpu.VMEM((9, POS + 2 * PAD, 3 * C1), F32)],
        size=4 << 20,
    )(cot, conv_second)
    blocks, keep = lax.optimization_barrier((blocks, keep))
    blocks = exchange(blocks, "dp")
    grad_z = call(hidden_grads, struct((POS, C1), BF16), spots(*[VMEM] * 4))(
        with_pair(pair), keep, with_cross(cross), zsum
    )
    grad_z = lax.all_gather(grad_z, "seq")

    half = struct((8, C1 // 16, 7 * 128), F32)
    keep, send = call(
        first_grads,
        (half, half),
        spots(VMEM, VMEM),
        [pltpu.VMEM((9 * D // 16, 18 * POS), BF16)],
    )(packed, grad_z)
    grad_first_half = keep
    for level in (1, 2, 3):
        half = struct((8 >> level, C1 // 16, 7 * 128), F32)
        came = swapped(send, STEPS[level - 1], "dp")
        sent = struct(half.shape, BF16 if level in (1, 2) else F32)
        keep, send = call(
            partial(half_sum, level), (half, sent), spots(VMEM, VMEM)
        )(keep, came)
    second = call(
        second_grads,
        struct((16, 48, 128), BF16),
        spots(VMEM, pl.ANY),
        [pltpu.VMEM((CO, 16 * POS), BF16), pltpu.VMEM((16 * POS, CO), BF16)],
        size=4 << 20,
    )(blocks, grad_first_half)
    grad_second = call(summed, struct((27, C1 // 16, CO // 16), F32), spots(VMEM))(
        exchange(second, "seq")
    )
    grad_second = grad_second.transpose(1, 2, 0)
    grad_first = call(last_sum, struct((27, C1 // 16, D // 16), F32), spots(VMEM, VMEM, pl.ANY))(
        keep, swapped(send, STEPS[3], "dp"), grad_second
    )
    return grad_first.transpose(0, 2, 1), grad_second.transpose(2, 0, 1)


def solution(mesh):
    return jax.shard_map(
        per_device,
        mesh=mesh,
        in_specs=(
            P("dp", "seq", None, None, None),
            P(),
            P(),
            P(),
            P(),
            P("dp", None, "seq", None, None),
            P("dp", None),
        ),
        out_specs=(P(None, "seq", "dp"), P(None, "seq", "dp")),
        check_vma=False,
    )
```
